512 devices in a mesh: dom: 32 (over z, x), band: 16 (over y, core).
Axes of the slice: x: 4, y: 8, z: 8, core: 2. Of those that a mesh axis runs over, the one named last changes fastest.
Arguments:
- waves: float32 [256, 131072], P('band', 'dom'), may hold values from -6 to 6
- potential: float32 [131072], P('dom'), may hold values from 0 to 4
- atom_points: int32 [128, 256], P('dom'), may hold values from 0 to 4095
- projectors: float32 [128, 8, 256], P('dom'), may hold values from -0.75 to 0.75
- coupling: float32 [128, 8, 8], P('dom'), may hold values from -1 to 1
Outputs:
- ortho: float32 [256, 131072], P('band', 'dom')
The draws below stay inside these ranges and needn't reach their ends.
Inputs may be any that keep to these rules, and one draw needn't show every extreme that they name: `atom_points`: an index of a point within the atom's own subdomain, repeats allowed.
All inputs are finite; a program needn't handle non-finite values.
Results may differ from the reference program's by a relative error of at most 0.0003.
Values sent between devices are 32-bit elements; how exact they have to be, the bound alone decides.
A program may use at most 64 MiB of HBM per device.

```python
import jax
import jax.numpy as jnp
from jax import lax

BANDS = 256
CUBE = 16
ATOM_DEV = 4
PTS = 256
PROJ = 8
GZ = 2
GY = 4
GX = 4
POINTS = 131072
ATOMS = 128
N_DOM = 32


def place_ends(entries, stream_key, low, high):
    longest = entries.shape.index(max(entries.shape))
    spots = []
    for shift in (0, 1):
        where = [jax.random.randint(jax.random.fold_in(stream_key, axis), (), 0, length) for axis, length in enumerate(entries.shape)]
        where[longest] = (where[longest] + shift) % entries.shape[longest]
        spots.append(tuple(where))
    return entries.at[spots[0]].set(low).at[spots[1]].set(high)


def block_levels(own_key, shape, shards, least, top_value):
    loudness, own = 1.0, jax.random.fold_in(own_key, 6)
    for dim, blocks in shards:
        heights = jnp.exp(jax.random.uniform(jax.random.fold_in(own, dim), (blocks,), jnp.float32, least / len(shards), top_value / len(shards)))
        loudness = loudness * jnp.repeat(heights, shape[dim] // blocks).reshape([-1 if axis == dim else 1 for axis in range(len(shape))])
    return loudness


def gaussian(stream_key, shape, scale, most, pieces=(), held_as=jnp.bfloat16):
    array = scale * jax.random.normal(stream_key, shape, jnp.float32)
    if pieces:
        array = array * block_levels(stream_key, shape, pieces, -0.22, 0.18)
    return jnp.clip(array, -most, most).astype(held_as)


def setup_inputs(seed: int = 0) -> dict:
    key_list = jax.random.split(jax.random.key(seed), 6)
    waves = gaussian(key_list[0], (BANDS, POINTS), 1.0, 6.0, ((0, 16), (1, 32)), jnp.float32)
    potential = jnp.clip(4.0 * jax.random.uniform(key_list[1], (POINTS,), jnp.float32) ** block_levels(key_list[1], (POINTS,), ((0, 32),), -0.2, 0.2), 0.0, 4.0)
    atom_points = place_ends(jax.random.randint(key_list[2], (ATOMS, PTS), 0, CUBE**3), jax.random.fold_in(key_list[2], 1), 0, (CUBE**3) - 1).astype(jnp.int32)
    projectors = gaussian(key_list[3], (ATOMS, PROJ, PTS), (PTS // 4) ** -0.5, 0.75, ((0, 32),), jnp.float32)
    coupling = jnp.clip(jax.random.uniform(key_list[4], (ATOMS, PROJ, PROJ), jnp.float32, -1.0, 1.0) * block_levels(key_list[4], (ATOMS, PROJ, PROJ), ((0, 32),), -0.4, 0.0), -1.0, 1.0)
    return dict(waves=waves, potential=potential, atom_points=atom_points, projectors=projectors, coupling=coupling)


high = lax.Precision.HIGHEST

def to_grid(flat):
    count = flat.shape[0]
    shaped = flat.reshape(count, GX, GY, GZ, CUBE, CUBE, CUBE)
    return shaped.transpose(0, 1, 4, 2, 5, 3, 6).reshape(count, GX * CUBE, GY * CUBE, GZ * CUBE)

def from_grid(grid):
    count = grid.shape[0]
    shaped = grid.reshape(count, GX, CUBE, GY, CUBE, GZ, CUBE)
    return shaped.transpose(0, 1, 3, 5, 2, 4, 6).reshape(count, -1)

def laplace(grid):
    padded = jnp.pad(grid, ((0, 0), (2, 2), (2, 2), (2, 2)))
    total = -7.5 * grid
    for axis in range(1, 4):
        size = grid.shape[axis]

        def part(offset):
            return lax.slice_in_dim(padded, offset, offset + size, axis=axis)
        other = [a for a in range(1, 4) if a != axis]
        near = part(1) + part(3)
        far = part(0) + part(4)
        for a in other:
            near = lax.slice_in_dim(near, 2, 2 + grid.shape[a], axis=a)
            far = lax.slice_in_dim(far, 2, 2 + grid.shape[a], axis=a)
        total = total + 4.0 / 3.0 * near - 1.0 / 12.0 * far
    return total

def nonlocal_one(values, points, proj, coup):
    picked = values[:, points]
    coef = jnp.einsum('aks,bas->bak', proj, picked, precision=high)
    mixed = jnp.einsum('akj,baj->bak', coup, coef, precision=high)
    spread = jnp.einsum('aks,bak->bas', proj, mixed, precision=high)
    return jnp.zeros_like(values).at[:, points.reshape(-1)].add(spread.reshape(values.shape[0], -1))

def apply_h(values, potential, atom_points, projectors, coupling):
    count = values.shape[0]
    kinetic = from_grid(laplace(to_grid(values)))
    per_dom = values.reshape(count, N_DOM, CUBE ** 3).transpose(1, 0, 2)
    points = atom_points.reshape(N_DOM, ATOM_DEV, PTS)
    proj = projectors.reshape(N_DOM, ATOM_DEV, PROJ, PTS)
    coup = coupling.reshape(N_DOM, ATOM_DEV, PROJ, PROJ)
    extra = lax.map(lambda z: nonlocal_one(z[0], z[1], z[2], z[3]), (per_dom, points, proj, coup))
    extra = extra.transpose(1, 0, 2).reshape(count, -1)
    return -0.5 * kinetic + potential[None, :] * values + extra

def reference(waves, potential, atom_points, projectors, coupling):
    first = (apply_h(waves, potential, atom_points, projectors, coupling) - 6.0 * waves) / 4.0
    filtered = 2.0 * (apply_h(first, potential, atom_points, projectors, coupling) - 6.0 * first) / 4.0 - waves
    gram = jnp.dot(filtered.astype(jnp.float32), filtered.T.astype(jnp.float32), precision=high, preferred_element_type=jnp.float32) / (N_DOM * CUBE ** 3)
    lower = jnp.linalg.cholesky(gram)
    return jax.scipy.linalg.solve_triangular(lower, filtered, lower=True)
```

```python
import jax
import jax.numpy as jnp
from jax import lax
from jax.experimental import pallas as pl
from jax.experimental.pallas import tpu as pltpu
from jax.sharding import PartitionSpec as P

F32, BF16 = jnp.float32, jnp.bfloat16
MESH = pl.DeviceIdType.MESH
CUBE = 16
BAND_LOC = 16
PLANE = CUBE * CUBE
POINTS = 131072
NBAND, NZ, NX = 16, 8, 4
ROWS = 17
BLOCK = 32


def iota(shape, dim):
    return lax.broadcasted_iota(jnp.int32, shape, dim)


def split(x):
    big = x.astype(BF16)
    return big, (x - big.astype(F32)).astype(BF16)


def dot(a, b, ca=1, cb=0):
    return lax.dot_general(a, b, (((ca,), (cb,)), ((), ())), preferred_element_type=F32)


def dot3(a, b, ca=1, cb=0):
    ah, al = split(a)
    bh, bl = split(b)
    return dot(ah, bh, ca, cb) + (dot(ah, bl, ca, cb) + dot(al, bh, ca, cb))


def bias(delta):
    step = jnp.abs(delta)
    return jnp.where(step == 1, -16.0, jnp.where(step == 2, 1.0, 0.0))


def kernel(
    waves, pot, pts, proj, coup, out,
    vx0, vx1, pterm, facesend, facerecv, pick, stencil, bhl, ecat, fs, work,
    ptv, projv, coupv, potv, part, rs_buf, z_buf, x_buf, g_buf,
    in_sem, h_send, h_recv, a_send, a_recv, r_send, r_recv, z_send, z_recv, x_send, x_recv,
    g_send, g_recv, o_send, o_recv, o_own,
):
    dom, band = lax.axis_index("dom"), lax.axis_index("band")
    pz, px = dom // NX, lax.rem(dom, NX)
    iz = lax.rem(dom, 2)
    iy = lax.rem(dom // 2, 4)
    ix = dom // 8
    middle = jnp.logical_or(iy == 1, iy == 2)

    copies = [
        pltpu.make_async_copy(
            waves.at[:, pl.ds(PLANE * i, PLANE)], vx0.at[pl.ds(32 + 16 * i, 16), :], in_sem.at[i]
        )
        for i in range(CUBE)
    ]
    small = [
        pltpu.make_async_copy(src, dst, in_sem.at[16 + i])
        for i, (src, dst) in enumerate(((pts, ptv), (proj, projv), (coup, coupv), (pot, potv)))
    ]
    for copy in copies + small:
        copy.start()

    facerecv[...] = jnp.zeros_like(facerecv)
    for ref in (vx0, vx1):
        ref[0:32, :] = jnp.zeros((32, PLANE), F32)
        ref[288:320, :] = jnp.zeros((32, PLANE), F32)

    barrier = pltpu.get_barrier_semaphore()

    def greet(where):
        pl.semaphore_signal(barrier, inc=1, device_id=where, device_id_type=MESH)

    @pl.loop(1, NBAND)
    def _(k):
        greet((dom, lax.rem(band + k, NBAND)))

    @pl.loop(1, NZ)
    def _(k):
        greet((lax.rem(pz + k, NZ) * NX + px, band))

    @pl.loop(1, NX)
    def _(k):
        greet((pz * NX + lax.rem(px + k, NX), band))

    @pl.when(iy == 1)
    def _():
        greet((dom + 2, band))

    @pl.when(iy == 2)
    def _():
        greet((dom - 2, band))

    row, col = iota((PLANE, 128), 0), iota((PLANE, 128), 1)
    ry, rz = row // 16, lax.rem(row, 16)
    cj, cp = lax.rem(col // 16, 2), lax.rem(col, 16)
    one, nil = jnp.float32(1), jnp.float32(0)
    zlo = jnp.where(iz == 0, 14, 0)
    pick[:, 0:128] = jnp.where(jnp.logical_and(ry == cj, rz == cp), one, nil).astype(BF16)
    pick[:, 128:256] = jnp.where(jnp.logical_and(ry == cj + 14, rz == cp), one, nil).astype(BF16)
    pick[:, 256:384] = jnp.where(jnp.logical_and(rz == cj + zlo, ry == cp), one, nil).astype(BF16)

    row, col = iota((PLANE, PLANE), 0), iota((PLANE, PLANE), 1)
    ry, rz, cy, cz = row // 16, lax.rem(row, 16), col // 16, lax.rem(col, 16)
    stencil[0:256, :] = (
        jnp.where(rz == cz, bias(ry - cy), 0.0) + jnp.where(ry == cy, bias(rz - cz), 0.0)
    ).astype(BF16)
    row, col = iota((128, PLANE), 0), iota((128, PLANE), 1)
    cy, cz = col // 16, lax.rem(col, 16)
    rj, rp = lax.rem(row // 16, 2), lax.rem(row, 16)
    stencil[256:384, :] = jnp.where(rp == cz, bias(rj - 2 - cy), 0.0).astype(BF16)
    stencil[384:512, :] = jnp.where(rp == cz, bias(rj + 16 - cy), 0.0).astype(BF16)
    zat = jnp.where(iz == 0, 16, -2)
    stencil[512:640, :] = jnp.where(rp == cy, bias(rj + zat - cz), 0.0).astype(BF16)

    for copy in small:
        copy.wait()

    for i in range(CUBE):
        line = potv[0:1, PLANE * i : PLANE * (i + 1)]
        pterm[16 * i : 16 * i + 16, :] = jnp.broadcast_to(0.25 * (line - 2.25), (16, PLANE))

    for a in range(4):
        where = ptv[a : a + 1, :]
        upper, lower = where // 128, lax.rem(where, 128)
        hot = jnp.where(iota((128, 256), 0) == lower, one, nil).astype(BF16)
        values = projv[a]
        spread = jnp.concatenate(
            [jnp.where(upper == h, values, nil) for h in range(32)], axis=0
        )
        s0, rest = split(spread)
        s1, s2 = split(spread - s0.astype(F32))
        dense = dot(s0, hot, 1, 1) + (dot(s1, hot, 1, 1) + dot(s2, hot, 1, 1))
        flat = jnp.concatenate([dense[8 * h : 8 * h + 8, :] for h in range(32)], axis=1)
        mixed = lax.dot_general(
            0.25 * coupv[a], flat, (((0,), (0,)), ((), ())),
            preferred_element_type=F32, precision=lax.Precision.HIGHEST,
        )
        fh, fl = split(flat)
        eh, el = split(mixed)
        bhl[8 * a : 8 * a + 8, :] = fh.astype(F32)
        bhl[32 + 8 * a : 40 + 8 * a, :] = fl.astype(F32)
        ecat[8 * a : 8 * a + 8, :] = eh.astype(F32)
        ecat[32 + 8 * a : 40 + 8 * a, :] = eh.astype(F32)
        ecat[64 + 8 * a : 72 + 8 * a, :] = el.astype(F32)

    for copy in copies:
        copy.wait()
    pl.semaphore_wait(barrier, 25 + middle.astype(jnp.int32))

    group = iota((64, 128), 1) // 32

    def halo(turn, ref):
        def face(slot, src, dst, where):
            return pltpu.make_async_remote_copy(
                src_ref=src, dst_ref=dst, send_sem=h_send.at[turn, slot],
                recv_sem=h_recv.at[turn, slot], device_id=(where, band), device_id_type=MESH,
            )
        return (
            (iy > 0, iy < 3, face(0, facesend.at[turn, 0], facerecv.at[turn, 1], dom - 2)),
            (iy < 3, iy > 0, face(1, facesend.at[turn, 1], facerecv.at[turn, 0], dom + 2)),
            (None, None, face(2, facesend.at[turn, 2], facerecv.at[turn, 2], dom + 1 - 2 * iz)),
            (ix > 0, ix < 3, face(3, ref.at[pl.ds(32, 32), :], ref.at[pl.ds(288, 32), :], dom - 8)),
            (ix < 3, ix > 0, face(4, ref.at[pl.ds(256, 32), :], ref.at[pl.ds(0, 32), :], dom + 8)),
        )

    def under(condition, action):
        if condition is None:
            action()
        else:
            pl.when(condition)(action)

    def apply(turn, ref):
        faces = halo(turn, ref)
        for slot in (3, 4):
            under(faces[slot][0], faces[slot][2].start)
        here = ref[32:288, :]
        vh, vl = split(here)
        ends = dot(vh, pick[...]) + dot(vl, pick[...])
        for slot in range(3):
            packed = ends[0:64, 128 * slot : 128 * slot + 128]
            for g in range(1, 4):
                packed = jnp.where(
                    group == g, ends[64 * g : 64 * g + 64, 128 * slot : 128 * slot + 128], packed
                )
            facesend[turn, slot] = packed
        for slot in (0, 1, 2):
            under(faces[slot][0], faces[slot][2].start)
        both = jnp.concatenate(
            [jnp.concatenate([v[16 * i : 16 * i + 16, :] for i in range(CUBE)], axis=1) for v in (vh, vl)],
            axis=0,
        )
        quad = dot(both, bhl[...].astype(BF16), 1, 1)
        coef = quad[0:16, 0:32] + (quad[0:16, 32:64] + quad[16:32, 0:32])
        ch, cl = split(coef)
        added = dot(jnp.concatenate([ch, cl, ch], axis=1), ecat[...].astype(BF16))
        added = jnp.concatenate([added[:, PLANE * i : PLANE * (i + 1)] for i in range(CUBE)], axis=0)
        inner = dot(vh, stencil[0:256, :]) + dot(vl, stencil[0:256, :])
        base = pterm[...] * here + added
        for face in faces:
            under(face[1], face[2].wait_recv)
        wide = jnp.concatenate(
            [
                jnp.concatenate(
                    [jnp.where(group == g, facerecv[turn, slot], 0.0) for g in range(4)], axis=0
                )
                for slot in range(3)
            ],
            axis=1,
        )
        wh, wl = split(wide)
        outer = dot(wh, stencil[256:640, :]) + dot(wl, stencil[256:640, :])
        far = ref[0:256, :] + ref[64:320, :]
        near = ref[16:272, :] + ref[48:304, :]
        return base + (1.0 / 96.0) * ((inner + outer) + (far - 16.0 * near))

    vx1[32:288, :] = apply(0, vx0)
    fs[...] = 2.0 * apply(1, vx1) - vx0[32:288, :]

    def to_piece(peer):
        return pltpu.make_async_remote_copy(
            src_ref=fs.at[pl.ds(pl.multiple_of(peer * 16, 16), 16), :],
            dst_ref=work.at[pl.ds(pl.multiple_of(band * 16, 16), 16), pl.ds(PLANE, PLANE)],
            send_sem=a_send.at[peer], recv_sem=a_recv.at[band],
            device_id=(dom, peer), device_id_type=MESH,
        )

    def from_piece(peer):
        return pltpu.make_async_remote_copy(
            src_ref=fs.at[pl.ds(0, 16), :],
            dst_ref=work.at[pl.ds(pl.multiple_of(peer * 16, 16), 16), pl.ds(PLANE, PLANE)],
            send_sem=a_send.at[peer], recv_sem=a_recv.at[peer],
            device_id=(dom, peer), device_id_type=MESH,
        )

    def peers(count, me, action):
        @pl.loop(1, count)
        def _(k):
            action(lax.rem(me + k, count))

    peers(NBAND, band, lambda peer: to_piece(peer).start())
    mine = pl.ds(pl.multiple_of(band * 16, 16), 16)
    work[mine, PLANE : 2 * PLANE] = fs[mine, :]
    peers(NBAND, band, lambda peer: from_piece(peer).wait_recv())

    piece = work[:, PLANE : 2 * PLANE]
    ph, plo = split(piece)
    gram = (1.0 / POINTS) * (dot(ph, ph, 1, 1) + (dot(ph, plo, 1, 1) + dot(plo, ph, 1, 1)))
    row, col = iota((128, 128), 0), iota((128, 128), 1)
    low = gram[128:256, 128:256]
    packed = jnp.where(row >= col, gram[0:128, 0:128], low)
    diag = jnp.sum(jnp.where(row == col, low, 0.0), axis=0, keepdims=True)
    for c in range(NBAND):
        part[c, 0:8, :] = packed[8 * c : 8 * c + 8, :]
        part[c, 8:16, :] = gram[128 + 8 * c : 136 + 8 * c, 0:128]
        part[c, 16:17, :] = diag

    def chunk(src, dst, send, recv, where):
        return pltpu.make_async_remote_copy(
            src_ref=src, dst_ref=dst, send_sem=send, recv_sem=recv, device_id=where, device_id_type=MESH
        )

    def at_band(peer):
        return (dom, peer)

    def at_z(peer):
        return (peer * NX + px, band)

    def at_x(peer):
        return (pz * NX + peer, band)

    def gather(count, me, at, own, buf, send, recv):
        peers(count, me, lambda peer: chunk(
            buf.at[me], buf.at[me], send.at[peer], recv.at[me], at(peer)).start())
        peers(count, me, lambda peer: chunk(
            buf.at[me], buf.at[peer], send.at[peer], recv.at[peer], at(peer)).wait_recv())

    def total(buf, count):
        value = buf[0]
        for i in range(1, count):
            value = value + buf[i]
        return value

    peers(NBAND, band, lambda peer: chunk(
        part.at[peer], rs_buf.at[band], r_send.at[peer], r_recv.at[band], at_band(peer)).start())
    rs_buf[band] = part[band]
    peers(NBAND, band, lambda peer: chunk(
        part.at[peer], rs_buf.at[peer], r_send.at[peer], r_recv.at[peer], at_band(peer)).wait_recv())
    z_buf[pz] = total(rs_buf, NBAND)
    gather(NZ, pz, at_z, None, z_buf, z_send, z_recv)
    x_buf[px] = total(z_buf, NZ)
    gather(NX, px, at_x, None, x_buf, x_send, x_recv)
    g_buf[band] = total(x_buf, NX)
    gather(NBAND, band, at_band, None, g_buf, g_send, g_recv)

    packed = jnp.concatenate([g_buf[c, 0:8, :] for c in range(NBAND)], axis=0)
    cross = jnp.concatenate([g_buf[c, 8:16, :] for c in range(NBAND)], axis=0)
    diag = jnp.broadcast_to(g_buf[0, 16:17, :], (128, 128))
    turned = packed.T
    work[0:128, 0:128] = jnp.where(row >= col, packed, turned)
    work[128:256, 128:256] = jnp.where(row < col, packed, jnp.where(row == col, diag, turned))
    work[128:256, 0:128] = cross
    work[0:128, 128:256] = cross.T

    def to_out(peer):
        return pltpu.make_async_remote_copy(
            src_ref=fs.at[pl.ds(pl.multiple_of(peer * 16, 16), 16), :],
            dst_ref=out.at[:, pl.ds(pl.multiple_of(band * PLANE, PLANE), PLANE)],
            send_sem=o_send.at[peer], recv_sem=o_recv.at[band],
            device_id=(dom, peer), device_id_type=MESH,
        )

    def from_out(peer):
        return pltpu.make_async_remote_copy(
            src_ref=fs.at[pl.ds(0, 16), :],
            dst_ref=out.at[:, pl.ds(pl.multiple_of(peer * PLANE, PLANE), PLANE)],
            send_sem=o_send.at[peer], recv_sem=o_recv.at[peer],
            device_id=(dom, peer), device_id_type=MESH,
        )

    peers(NBAND, band, lambda peer: to_piece(peer).wait_send())

    brow, bcol = iota((BLOCK, 128), 0), iota((BLOCK, 128), 1)
    lane = iota((BLOCK, 256), 1)

    @pl.loop(0, 256 // BLOCK)
    def _(j):
        first = pl.multiple_of(j * BLOCK, BLOCK)
        rows = work[pl.ds(first, BLOCK), :]
        turned = pltpu.roll(rows[:, 0:256], lax.rem(256 + BLOCK - first, 256), 1)
        x = jnp.where(bcol < BLOCK, jnp.where(brow == bcol, 1.0, 0.0), turned[:, 0:128])
        for k in range(BLOCK - 1):
            pivot = x[k : k + 1, :]
            factor = x[:, BLOCK + k : BLOCK + k + 1] * (1.0 / pivot[:, BLOCK + k : BLOCK + k + 1])
            x = x - jnp.where(brow > k, factor, 0.0) * pivot
        d = jnp.sum(jnp.where(bcol == brow + BLOCK, x, 0.0), axis=1, keepdims=True)
        inverse = (x * lax.rsqrt(d))[:, 0:BLOCK]
        done = dot3(inverse, rows)
        fs[pl.ds(first, BLOCK), :] = done[:, 256:512]
        for half in range(BLOCK // 16):
            peer = j * (BLOCK // 16) + half

            @pl.when(peer != band)
            def _():
                to_out(peer).start()

        left = jnp.where(lane >= first + BLOCK, done[:, 0:256], 0.0)
        work[...] = work[...] - dot3(left, done, 0, 0)

    own = pltpu.make_async_copy(
        fs.at[mine, :], out.at[:, pl.ds(pl.multiple_of(band * PLANE, PLANE), PLANE)], o_own
    )
    own.start()
    for turn, ref in ((0, vx0), (1, vx1)):
        for face in halo(turn, ref):
            under(face[0], face[2].wait_send)
    peers(NBAND, band, lambda peer: chunk(
        part.at[peer], rs_buf.at[peer], r_send.at[peer], r_recv.at[peer], at_band(peer)).wait_send())
    for count, me, at, buf, send, recv in (
        (NZ, pz, at_z, z_buf, z_send, z_recv),
        (NX, px, at_x, x_buf, x_send, x_recv),
        (NBAND, band, at_band, g_buf, g_send, g_recv),
    ):
        peers(count, me, lambda peer: chunk(
            buf.at[me], buf.at[peer], send.at[peer], recv.at[peer], at(peer)).wait_send())
    peers(NBAND, band, lambda peer: from_out(peer).wait_recv())
    peers(NBAND, band, lambda peer: to_out(peer).wait_send())
    own.wait()


def local(waves, potential, atom_points, projectors, coupling):
    dma = pltpu.SemaphoreType.DMA
    vmem = pltpu.VMEM
    return pl.pallas_call(
        kernel,
        out_shape=jax.ShapeDtypeStruct((BAND_LOC, CUBE**3), F32),
        in_specs=[pl.BlockSpec(memory_space=pl.ANY)] * 5,
        out_specs=pl.BlockSpec(memory_space=pl.ANY),
        scratch_shapes=[
            vmem((320, 256), F32), vmem((320, 256), F32), vmem((256, 256), F32),
            vmem((2, 3, 64, 128), F32), vmem((2, 3, 64, 128), F32),
            vmem((256, 384), BF16), vmem((640, 256), BF16),
            vmem((64, 4096), F32), vmem((96, 4096), F32),
            vmem((256, 256), F32), vmem((256, 512), F32),
            vmem((4, 256), jnp.int32), vmem((4, 8, 256), F32), vmem((4, 8, 8), F32), vmem((1, 4096), F32),
            vmem((NBAND, ROWS, 128), F32), vmem((NBAND, ROWS, 128), F32),
            vmem((NZ, ROWS, 128), F32), vmem((NX, ROWS, 128), F32), vmem((NBAND, ROWS, 128), F32),
            dma((20,)), dma((2, 5)), dma((2, 5)), dma((16,)), dma((16,)), dma((16,)), dma((16,)),
            dma((8,)), dma((8,)), dma((4,)), dma((4,)), dma((16,)), dma((16,)), dma((16,)), dma((16,)),
            dma,
        ],
        compiler_params=pltpu.CompilerParams(collective_id=0, has_side_effects=True),
    )(waves, potential.reshape(1, CUBE**3), atom_points, projectors, coupling)


def solution(mesh):
    placed = (
        P("band", "dom"),
        P("dom"),
        P("dom", None),
        P("dom", None, None),
        P("dom", None, None),
    )
    return jax.shard_map(
        local, mesh=mesh, in_specs=placed, out_specs=P("band", "dom"), check_vma=False
    )
```

```python
import jax
import jax.numpy as jnp
from jax import lax
from jax.experimental import pallas as pl
from jax.experimental.pallas import tpu as pltpu
from jax.sharding import PartitionSpec as P

F32, BF16 = jnp.float32, jnp.bfloat16
MESH = pl.DeviceIdType.MESH
CUBE = 16
BAND_LOC = 16
PLANE = CUBE * CUBE
POINTS = 131072
NBAND, NZ, NX = 16, 8, 4
ROWS = 17
BLOCK = 32


def iota(shape, dim):
    return lax.broadcasted_iota(jnp.int32, shape, dim)


def split(x):
    big = x.astype(BF16)
    return big, (x - big.astype(F32)).astype(BF16)


def dot(a, b, ca=1, cb=0):
    return lax.dot_general(a, b, (((ca,), (cb,)), ((), ())), preferred_element_type=F32)


def dot3(a, b, ca=1, cb=0):
    ah, al = split(a)
    bh, bl = split(b)
    return dot(ah, bh, ca, cb) + (dot(ah, bl, ca, cb) + dot(al, bh, ca, cb))


def bias(delta):
    step = jnp.abs(delta)
    return jnp.where(step == 1, -16.0, jnp.where(step == 2, 1.0, 0.0))


def kernel(
    waves, pot, pts, proj, coup, out,
    vx0, vx1, pterm, facesend, facerecv, pick, stencil, bhl, ecat, fs, work,
    ptv, projv, coupv, potv, part, rs_buf, z_buf, x_buf, g_buf,
    in_sem, h_send, h_recv, a_send, a_recv, r_send, r_recv, z_send, z_recv, x_send, x_recv,
    g_send, g_recv, o_send, o_recv, o_own,
):
    dom, band = lax.axis_index("dom"), lax.axis_index("band")
    pz, px = dom // NX, lax.rem(dom, NX)
    iz = lax.rem(dom, 2)
    iy = lax.rem(dom // 2, 4)
    ix = dom // 8
    middle = jnp.logical_or(iy == 1, iy == 2)

    copies = [
        pltpu.make_async_copy(
            waves.at[:, pl.ds(PLANE * i, PLANE)], vx0.at[pl.ds(32 + 16 * i, 16), :], in_sem.at[i]
        )
        for i in range(CUBE)
    ]
    small = [
        pltpu.make_async_copy(src, dst, in_sem.at[16 + i])
        for i, (src, dst) in enumerate(((pts, ptv), (proj, projv), (coup, coupv), (pot, potv)))
    ]
    for copy in copies + small:
        copy.start()

    facerecv[...] = jnp.zeros_like(facerecv)
    for ref in (vx0, vx1):
        ref[0:32, :] = jnp.zeros((32, PLANE), F32)
        ref[288:320, :] = jnp.zeros((32, PLANE), F32)

    barrier = pltpu.get_barrier_semaphore()

    def greet(where):
        pl.semaphore_signal(barrier, inc=1, device_id=where, device_id_type=MESH)

    @pl.loop(1, NBAND)
    def _(k):
        greet((dom, lax.rem(band + k, NBAND)))

    @pl.loop(1, NZ)
    def _(k):
        greet((lax.rem(pz + k, NZ) * NX + px, band))

    @pl.loop(1, NX)
    def _(k):
        greet((pz * NX + lax.rem(px + k, NX), band))

    @pl.when(iy == 1)
    def _():
        greet((dom + 2, band))

    @pl.when(iy == 2)
    def _():
        greet((dom - 2, band))

    row, col = iota((PLANE, 128), 0), iota((PLANE, 128), 1)
    ry, rz = row // 16, lax.rem(row, 16)
    cj, cp = lax.rem(col // 16, 2), lax.rem(col, 16)
    one, nil = jnp.float32(1), jnp.float32(0)
    zlo = jnp.where(iz == 0, 14, 0)
    pick[:, 0:128] = jnp.where(jnp.logical_and(ry == cj, rz == cp), one, nil).astype(BF16)
    pick[:, 128:256] = jnp.where(jnp.logical_and(ry == cj + 14, rz == cp), one, nil).astype(BF16)
    pick[:, 256:384] = jnp.where(jnp.logical_and(rz == cj + zlo, ry == cp), one, nil).astype(BF16)

    row, col = iota((PLANE, PLANE), 0), iota((PLANE, PLANE), 1)
    ry, rz, cy, cz = row // 16, lax.rem(row, 16), col // 16, lax.rem(col, 16)
    stencil[0:256, :] = (
        jnp.where(rz == cz, bias(ry - cy), 0.0) + jnp.where(ry == cy, bias(rz - cz), 0.0)
    ).astype(BF16)
    row, col = iota((128, PLANE), 0), iota((128, PLANE), 1)
    cy, cz = col // 16, lax.rem(col, 16)
    rj, rp = lax.rem(row // 16, 2), lax.rem(row, 16)
    stencil[256:384, :] = jnp.where(rp == cz, bias(rj - 2 - cy), 0.0).astype(BF16)
    stencil[384:512, :] = jnp.where(rp == cz, bias(rj + 16 - cy), 0.0).astype(BF16)
    zat = jnp.where(iz == 0, 16, -2)
    stencil[512:640, :] = jnp.where(rp == cy, bias(rj + zat - cz), 0.0).astype(BF16)

    for copy in small:
        copy.wait()

    for i in range(CUBE):
        line = potv[0:1, PLANE * i : PLANE * (i + 1)]
        pterm[16 * i : 16 * i + 16, :] = jnp.broadcast_to(0.25 * (line - 2.25), (16, PLANE))

    for a in range(4):
        where = ptv[a : a + 1, :]
        upper, lower = where // 128, lax.rem(where, 128)
        hot = jnp.where(iota((128, 256), 0) == lower, one, nil).astype(BF16)
        values = projv[a]
        spread = jnp.concatenate(
            [jnp.where(upper == h, values, nil) for h in range(32)], axis=0
        )
        s0, rest = split(spread)
        s1, s2 = split(spread - s0.astype(F32))
        dense = dot(s0, hot, 1, 1) + (dot(s1, hot, 1, 1) + dot(s2, hot, 1, 1))
        flat = jnp.concatenate([dense[8 * h : 8 * h + 8, :] for h in range(32)], axis=1)
        mixed = lax.dot_general(
            0.25 * coupv[a], flat, (((0,), (0,)), ((), ())),
            preferred_element_type=F32, precision=lax.Precision.HIGHEST,
        )
        fh, fl = split(flat)
        eh, el = split(mixed)
        bhl[8 * a : 8 * a + 8, :] = fh.astype(F32)
        bhl[32 + 8 * a : 40 + 8 * a, :] = fl.astype(F32)
        ecat[8 * a : 8 * a + 8, :] = eh.astype(F32)
        ecat[32 + 8 * a : 40 + 8 * a, :] = eh.astype(F32)
        ecat[64 + 8 * a : 72 + 8 * a, :] = el.astype(F32)

    for copy in copies:
        copy.wait()
    pl.semaphore_wait(barrier, 25 + middle.astype(jnp.int32))

    group = iota((64, 128), 1) // 32

    def halo(turn, ref):
        def face(slot, src, dst, where):
            return pltpu.make_async_remote_copy(
                src_ref=src, dst_ref=dst, send_sem=h_send.at[turn, slot],
                recv_sem=h_recv.at[turn, slot], device_id=(where, band), device_id_type=MESH,
            )
        return (
            (iy > 0, iy < 3, face(0, facesend.at[turn, 0], facerecv.at[turn, 1], dom - 2)),
            (iy < 3, iy > 0, face(1, facesend.at[turn, 1], facerecv.at[turn, 0], dom + 2)),
            (None, None, face(2, facesend.at[turn, 2], facerecv.at[turn, 2], dom + 1 - 2 * iz)),
            (ix > 0, ix < 3, face(3, ref.at[pl.ds(32, 32), :], ref.at[pl.ds(288, 32), :], dom - 8)),
            (ix < 3, ix > 0, face(4, ref.at[pl.ds(256, 32), :], ref.at[pl.ds(0, 32), :], dom + 8)),
        )

    def under(condition, action):
        if condition is None:
            action()
        else:
            pl.when(condition)(action)

    def apply(turn, ref):
        faces = halo(turn, ref)
        for slot in (3, 4):
            under(faces[slot][0], faces[slot][2].start)
        here = ref[32:288, :]
        vh, vl = split(here)
        ends = dot(vh, pick[...]) + dot(vl, pick[...])
        for slot in range(3):
            packed = ends[0:64, 128 * slot : 128 * slot + 128]
            for g in range(1, 4):
                packed = jnp.where(
                    group == g, ends[64 * g : 64 * g + 64, 128 * slot : 128 * slot + 128], packed
                )
            facesend[turn, slot] = packed
        for slot in (0, 1, 2):
            under(faces[slot][0], faces[slot][2].start)
        both = jnp.concatenate(
            [jnp.concatenate([v[16 * i : 16 * i + 16, :] for i in range(CUBE)], axis=1) for v in (vh, vl)],
            axis=0,
        )
        quad = dot(both, bhl[...].astype(BF16), 1, 1)
        coef = quad[0:16, 0:32] + (quad[0:16, 32:64] + quad[16:32, 0:32])
        ch, cl = split(coef)
        added = dot(jnp.concatenate([ch, cl, ch], axis=1), ecat[...].astype(BF16))
        added = jnp.concatenate([added[:, PLANE * i : PLANE * (i + 1)] for i in range(CUBE)], axis=0)
        inner = dot(vh, stencil[0:256, :]) + dot(vl, stencil[0:256, :])
        base = pterm[...] * here + added
        for face in faces:
            under(face[1], face[2].wait_recv)
        wide = jnp.concatenate(
            [
                jnp.concatenate(
                    [jnp.where(group == g, facerecv[turn, slot], 0.0) for g in range(4)], axis=0
                )
                for slot in range(3)
            ],
            axis=1,
        )
        wh, wl = split(wide)
        outer = dot(wh, stencil[256:640, :]) + dot(wl, stencil[256:640, :])
        far = ref[0:256, :] + ref[64:320, :]
        near = ref[16:272, :] + ref[48:304, :]
        return base + (1.0 / 96.0) * ((inner + outer) + (far - 16.0 * near))

    vx1[32:288, :] = apply(0, vx0)
    fs[...] = 2.0 * apply(1, vx1) - vx0[32:288, :]

    def to_piece(peer):
        return pltpu.make_async_remote_copy(
            src_ref=fs.at[pl.ds(pl.multiple_of(peer * 16, 16), 16), :],
            dst_ref=work.at[pl.ds(pl.multiple_of(band * 16, 16), 16), pl.ds(PLANE, PLANE)],
            send_sem=a_send.at[peer], recv_sem=a_recv.at[band],
            device_id=(dom, peer), device_id_type=MESH,
        )

    def from_piece(peer):
        return pltpu.make_async_remote_copy(
            src_ref=fs.at[pl.ds(0, 16), :],
            dst_ref=work.at[pl.ds(pl.multiple_of(peer * 16, 16), 16), pl.ds(PLANE, PLANE)],
            send_sem=a_send.at[peer], recv_sem=a_recv.at[peer],
            device_id=(dom, peer), device_id_type=MESH,
        )

    def peers(count, me, action):
        @pl.loop(1, count)
        def _(k):
            action(lax.rem(me + k, count))

    peers(NBAND, band, lambda peer: to_piece(peer).start())
    mine = pl.ds(pl.multiple_of(band * 16, 16), 16)
    work[mine, PLANE : 2 * PLANE] = fs[mine, :]
    peers(NBAND, band, lambda peer: from_piece(peer).wait_recv())

    piece = work[:, PLANE : 2 * PLANE]
    ph, plo = split(piece)
    gram = (1.0 / POINTS) * (dot(ph, ph, 1, 1) + (dot(ph, plo, 1, 1) + dot(plo, ph, 1, 1)))
    row, col = iota((128, 128), 0), iota((128, 128), 1)
    low = gram[128:256, 128:256]
    packed = jnp.where(row >= col, gram[0:128, 0:128], low)
    diag = jnp.sum(jnp.where(row == col, low, 0.0), axis=0, keepdims=True)
    for c in range(NBAND):
        part[c, 0:8, :] = packed[8 * c : 8 * c + 8, :]
        part[c, 8:16, :] = gram[128 + 8 * c : 136 + 8 * c, 0:128]
        part[c, 16:17, :] = diag

    def chunk(src, dst, send, recv, where):
        return pltpu.make_async_remote_copy(
            src_ref=src, dst_ref=dst, send_sem=send, recv_sem=recv, device_id=where, device_id_type=MESH
        )

    def at_band(peer):
        return (dom, peer)

    def at_z(peer):
        return (peer * NX + px, band)

    def at_x(peer):
        return (pz * NX + peer, band)

    def gather(count, me, at, own, buf, send, recv):
        peers(count, me, lambda peer: chunk(
            buf.at[me], buf.at[me], send.at[peer], recv.at[me], at(peer)).start())
        peers(count, me, lambda peer: chunk(
            buf.at[me], buf.at[peer], send.at[peer], recv.at[peer], at(peer)).wait_recv())

    def total(buf, count):
        value = buf[0]
        for i in range(1, count):
            value = value + buf[i]
        return value

    peers(NBAND, band, lambda peer: chunk(
        part.at[peer], rs_buf.at[band], r_send.at[peer], r_recv.at[band], at_band(peer)).start())
    rs_buf[band] = part[band]
    peers(NBAND, band, lambda peer: chunk(
        part.at[peer], rs_buf.at[peer], r_send.at[peer], r_recv.at[peer], at_band(peer)).wait_recv())
    z_buf[pz] = total(rs_buf, NBAND)
    gather(NZ, pz, at_z, None, z_buf, z_send, z_recv)
    x_buf[px] = total(z_buf, NZ)
    gather(NX, px, at_x, None, x_buf, x_send, x_recv)
    g_buf[band] = total(x_buf, NX)
    gather(NBAND, band, at_band, None, g_buf, g_send, g_recv)

    packed = jnp.concatenate([g_buf[c, 0:8, :] for c in range(NBAND)], axis=0)
    cross = jnp.concatenate([g_buf[c, 8:16, :] for c in range(NBAND)], axis=0)
    diag = jnp.broadcast_to(g_buf[0, 16:17, :], (128, 128))
    turned = packed.T
    work[0:128, 0:128] = jnp.where(row >= col, packed, turned)
    work[128:256, 128:256] = jnp.where(row < col, packed, jnp.where(row == col, diag, turned))
    work[128:256, 0:128] = cross
    work[0:128, 128:256] = cross.T

    def to_out(peer):
        return pltpu.make_async_remote_copy(
            src_ref=fs.at[pl.ds(pl.multiple_of(peer * 16, 16), 16), :],
            dst_ref=out.at[:, pl.ds(pl.multiple_of(band * PLANE, PLANE), PLANE)],
            send_sem=o_send.at[peer], recv_sem=o_recv.at[band],
            device_id=(dom, peer), device_id_type=MESH,
        )

    def from_out(peer):
        return pltpu.make_async_remote_copy(
            src_ref=fs.at[pl.ds(0, 16), :],
            dst_ref=out.at[:, pl.ds(pl.multiple_of(peer * PLANE, PLANE), PLANE)],
            send_sem=o_send.at[peer], recv_sem=o_recv.at[peer],
            device_id=(dom, peer), device_id_type=MESH,
        )

    peers(NBAND, band, lambda peer: to_piece(peer).wait_send())

    srow = iota((8, 128), 0)

    def spread_row(value, k):
        return jnp.broadcast_to(value[k : k + 1, :], (8, 128))

    for j in range(256 // BLOCK):
        first = j * BLOCK
        lo = first // 128 * 128
        count = BLOCK // 8
        tiles = [
            [work[first + 8 * t : first + 8 * t + 8, c : c + 128] for c in range(lo, 512, 128)]
            for t in range(count)
        ]
        for s in range(count):
            at = first - lo + 8 * s
            cols = {
                t: [jnp.broadcast_to(tiles[t][0][:, at + k : at + k + 1], (8, 128)) for k in range(8)]
                for t in range(s, count)
            }
            pivots = cols[s][0]
            for k in range(8):
                inverse = 1.0 / spread_row(cols[s][k], k)
                pivots = jnp.where(srow == k, cols[s][k], pivots)
                heads = {m: spread_row(cols[s][m], k) for m in range(k + 1, 8)}
                lead = [spread_row(v, k) for v in tiles[s]]
                for t in range(s, count):
                    if t == s and k == 7:
                        continue
                    factor = cols[t][k] * inverse
                    if t == s:
                        factor = jnp.where(srow > k, factor, 0.0)
                    for m in range(k + 1, 8):
                        cols[t][m] = cols[t][m] - factor * heads[m]
                    tiles[t] = [v - factor * r for v, r in zip(tiles[t], lead)]
            scale = lax.rsqrt(pivots)
            tiles[s] = [v * scale for v in tiles[s]]
        lanes = [jnp.concatenate([tiles[t][c] for t in range(count)], axis=0) for c in range((512 - lo) // 128)]
        fs[first : first + BLOCK, 0:128] = lanes[-2]
        fs[first : first + BLOCK, 128:256] = lanes[-1]
        for half in range(BLOCK // 16):
            peer = j * (BLOCK // 16) + half

            @pl.when(peer != band)
            def _():
                to_out(peer).start()

        after = first + BLOCK
        if after < 256:
            base = after // 128 * 128
            rest = jnp.concatenate(lanes[(base - lo) // 128 :], axis=1)
            left = rest[:, 0 : 256 - base].T
            update = dot3(left, rest)
            work[after:256, base:512] = work[after:256, base:512] - update[after - base :, :]

    own = pltpu.make_async_copy(
        fs.at[mine, :], out.at[:, pl.ds(pl.multiple_of(band * PLANE, PLANE), PLANE)], o_own
    )
    own.start()
    for turn, ref in ((0, vx0), (1, vx1)):
        for face in halo(turn, ref):
            under(face[0], face[2].wait_send)
    peers(NBAND, band, lambda peer: chunk(
        part.at[peer], rs_buf.at[peer], r_send.at[peer], r_recv.at[peer], at_band(peer)).wait_send())
    for count, me, at, buf, send, recv in (
        (NZ, pz, at_z, z_buf, z_send, z_recv),
        (NX, px, at_x, x_buf, x_send, x_recv),
        (NBAND, band, at_band, g_buf, g_send, g_recv),
    ):
        peers(count, me, lambda peer: chunk(
            buf.at[me], buf.at[peer], send.at[peer], recv.at[peer], at(peer)).wait_send())
    peers(NBAND, band, lambda peer: from_out(peer).wait_recv())
    peers(NBAND, band, lambda peer: to_out(peer).wait_send())
    own.wait()


def local(waves, potential, atom_points, projectors, coupling):
    dma = pltpu.SemaphoreType.DMA
    vmem = pltpu.VMEM
    return pl.pallas_call(
        kernel,
        out_shape=jax.ShapeDtypeStruct((BAND_LOC, CUBE**3), F32),
        in_specs=[pl.BlockSpec(memory_space=pl.ANY)] * 5,
        out_specs=pl.BlockSpec(memory_space=pl.ANY),
        scratch_shapes=[
            vmem((320, 256), F32), vmem((320, 256), F32), vmem((256, 256), F32),
            vmem((2, 3, 64, 128), F32), vmem((2, 3, 64, 128), F32),
            vmem((256, 384), BF16), vmem((640, 256), BF16),
            vmem((64, 4096), F32), vmem((96, 4096), F32),
            vmem((256, 256), F32), vmem((256, 512), F32),
            vmem((4, 256), jnp.int32), vmem((4, 8, 256), F32), vmem((4, 8, 8), F32), vmem((1, 4096), F32),
            vmem((NBAND, ROWS, 128), F32), vmem((NBAND, ROWS, 128), F32),
            vmem((NZ, ROWS, 128), F32), vmem((NX, ROWS, 128), F32), vmem((NBAND, ROWS, 128), F32),
            dma((20,)), dma((2, 5)), dma((2, 5)), dma((16,)), dma((16,)), dma((16,)), dma((16,)),
            dma((8,)), dma((8,)), dma((4,)), dma((4,)), dma((16,)), dma((16,)), dma((16,)), dma((16,)),
            dma,
        ],
        compiler_params=pltpu.CompilerParams(collective_id=0, has_side_effects=True),
    )(waves, potential.reshape(1, CUBE**3), atom_points, projectors, coupling)


def solution(mesh):
    placed = (
        P("band", "dom"),
        P("dom"),
        P("dom", None),
        P("dom", None, None),
        P("dom", None, None),
    )
    return jax.shard_map(
        local, mesh=mesh, in_specs=placed, out_specs=P("band", "dom"), check_vma=False
    )
```

```python
import jax
import jax.numpy as jnp
from jax import lax
from jax.experimental import pallas as pl
from jax.experimental.pallas import tpu as pltpu
from jax.sharding import PartitionSpec as P

F32, BF16 = jnp.float32, jnp.bfloat16
MESH = pl.DeviceIdType.MESH
CUBE = 16
BAND_LOC = 16
PLANE = CUBE * CUBE
POINTS = 131072
NBAND, NZ, NY, NX, NSET = 16, 8, 8, 4, 8
ROWS = 33
BLOCK = 32


def iota(shape, dim):
    return lax.broadcasted_iota(jnp.int32, shape, dim)


def split(x):
    big = x.astype(BF16)
    return big, (x - big.astype(F32)).astype(BF16)


def dot(a, b, ca=1, cb=0):
    return lax.dot_general(a, b, (((ca,), (cb,)), ((), ())), preferred_element_type=F32)


def bias(delta):
    step = jnp.abs(delta)
    return jnp.where(step == 1, -16.0, jnp.where(step == 2, 1.0, 0.0))


def kernel(
    waves, pot, pts, proj, coup, out,
    vx0, vx1, pterm, facesend, facerecv, pick, stencil, bhl, ecat, fs, work,
    ptv, projv, coupv, potv, part, rs_buf, ay_buf, az_buf, bz_buf, by_buf, g_buf,
    in_sem, h_send, h_recv, a_send, a_recv, r_send, r_recv, s_send, s_recv, o_send, o_recv, o_own,
):
    dom, band = lax.axis_index("dom"), lax.axis_index("band")
    pz, px = dom // NX, lax.rem(dom, NX)
    py, core = band // 2, lax.rem(band, 2)
    mine_set = px * 2 + core
    iz = lax.rem(dom, 2)
    iy = lax.rem(dom // 2, 4)
    ix = dom // 8
    middle = jnp.logical_or(iy == 1, iy == 2)

    copies = [
        pltpu.make_async_copy(
            waves.at[:, pl.ds(PLANE * i, PLANE)], vx0.at[pl.ds(32 + 16 * i, 16), :], in_sem.at[i]
        )
        for i in range(CUBE)
    ]
    small = [
        pltpu.make_async_copy(src, dst, in_sem.at[16 + i])
        for i, (src, dst) in enumerate(((pts, ptv), (proj, projv), (coup, coupv), (pot, potv)))
    ]
    for copy in copies + small:
        copy.start()

    facerecv[...] = jnp.zeros_like(facerecv)
    for ref in (vx0, vx1):
        ref[0:32, :] = jnp.zeros((32, PLANE), F32)
        ref[288:320, :] = jnp.zeros((32, PLANE), F32)

    def at_band(peer):
        return (dom, peer)

    def at_y(peer):
        return (dom, peer * 2 + core)

    def at_z(peer):
        return (peer * NX + px, band)

    def at_set(peer):
        return (pz * NX + peer // 2, py * 2 + lax.rem(peer, 2))

    barrier = pltpu.get_barrier_semaphore()

    def greet(where):
        pl.semaphore_signal(barrier, inc=1, device_id=where, device_id_type=MESH)

    @pl.loop(1, NBAND)
    def _(k):
        greet((dom, lax.rem(band + k, NBAND)))

    @pl.loop(1, NZ)
    def _(k):
        greet((lax.rem(pz + k, NZ) * NX + px, band))

    @pl.loop(1, NSET)
    def _(k):
        greet(at_set(lax.rem(mine_set + k, NSET)))

    @pl.when(iy == 1)
    def _():
        greet((dom + 2, band))

    @pl.when(iy == 2)
    def _():
        greet((dom - 2, band))

    group = iota((64, 128), 1) >> 5

    def halo(turn, ref):
        def face(slot, src, dst, where):
            return pltpu.make_async_remote_copy(
                src_ref=src, dst_ref=dst, send_sem=h_send.at[turn, slot],
                recv_sem=h_recv.at[turn, slot], device_id=(where, band), device_id_type=MESH,
            )
        return (
            (iy > 0, iy < 3, face(0, facesend.at[turn, 0], facerecv.at[turn, 1], dom - 2)),
            (iy < 3, iy > 0, face(1, facesend.at[turn, 1], facerecv.at[turn, 0], dom + 2)),
            (None, None, face(2, facesend.at[turn, 2], facerecv.at[turn, 2], dom + 1 - 2 * iz)),
            (ix > 0, ix < 3, face(3, ref.at[pl.ds(32, 32), :], ref.at[pl.ds(288, 32), :], dom - 8)),
            (ix < 3, ix > 0, face(4, ref.at[pl.ds(256, 32), :], ref.at[pl.ds(0, 32), :], dom + 8)),
        )

    def under(condition, action):
        if condition is None:
            action()
        else:
            pl.when(condition)(action)

    def pack_faces(turn, ref):
        vh, vl = split(ref[32:288, :])
        ends = dot(vh, pick[...]) + dot(vl, pick[...])
        for slot in range(3):
            packed = ends[0:64, 128 * slot : 128 * slot + 128]
            for g in range(1, 4):
                packed = jnp.where(
                    group == g, ends[64 * g : 64 * g + 64, 128 * slot : 128 * slot + 128], packed
                )
            facesend[turn, slot] = packed

    def send_faces(turn, ref, slots):
        faces = halo(turn, ref)
        for slot in slots:
            under(faces[slot][0], faces[slot][2].start)

    def inside(ref):
        here = ref[32:288, :]
        vh, vl = split(here)
        both = jnp.concatenate(
            [jnp.concatenate([v[16 * i : 16 * i + 16, :] for i in range(CUBE)], axis=1) for v in (vh, vl)],
            axis=0,
        )
        quad = dot(both, bhl[...].astype(BF16), 1, 1)
        coef = quad[0:16, 0:32] + (quad[0:16, 32:64] + quad[16:32, 0:32])
        ch, cl = split(coef)
        added = dot(jnp.concatenate([ch, cl, ch], axis=1), ecat[...].astype(BF16))
        added = jnp.concatenate([added[:, PLANE * i : PLANE * (i + 1)] for i in range(CUBE)], axis=0)
        inner = dot(vh, stencil[0:256, :]) + dot(vl, stencil[0:256, :])
        return pterm[...] * here + added + (1.0 / 96.0) * inner

    def outside(turn, ref):
        for face in halo(turn, ref):
            under(face[1], face[2].wait_recv)
        wide = jnp.concatenate(
            [
                jnp.concatenate(
                    [jnp.where(group == g, facerecv[turn, slot], 0.0) for g in range(4)], axis=0
                )
                for slot in range(3)
            ],
            axis=1,
        )
        wh, wl = split(wide)
        outer = dot(wh, stencil[256:640, :]) + dot(wl, stencil[256:640, :])
        far = ref[0:256, :] + ref[64:320, :]
        near = ref[16:272, :] + ref[48:304, :]
        return (1.0 / 96.0) * (outer + (far - 16.0 * near))

    row, col = iota((PLANE, 128), 0), iota((PLANE, 128), 1)
    ry, rz = row >> 4, row & 15
    cj, cp = (col >> 4) & 1, col & 15
    one, nil = jnp.float32(1), jnp.float32(0)
    zlo = jnp.where(iz == 0, 14, 0)
    pick[:, 0:128] = jnp.where(row == (col & 31), one, nil).astype(BF16)
    pick[:, 128:256] = jnp.where(row == (col & 31) + 224, one, nil).astype(BF16)
    pick[:, 256:384] = jnp.where(row == cp * 16 + cj + zlo, one, nil).astype(BF16)

    for copy in copies:
        copy.wait()
    pack_faces(0, vx0)
    pl.semaphore_wait(barrier, 29 + middle.astype(jnp.int32))
    send_faces(0, vx0, range(5))

    row, col = iota((PLANE, PLANE), 0), iota((PLANE, PLANE), 1)
    ry, rz, cy, cz = row >> 4, row & 15, col >> 4, col & 15
    stencil[0:256, :] = (
        jnp.where(rz == cz, bias(ry - cy), 0.0) + jnp.where(ry == cy, bias(rz - cz), 0.0)
    ).astype(BF16)
    row, col = iota((128, PLANE), 0), iota((128, PLANE), 1)
    cy, cz = col >> 4, col & 15
    rj, rp = (row >> 4) & 1, row & 15
    stencil[256:384, :] = jnp.where(rp == cz, bias(rj - 2 - cy), 0.0).astype(BF16)
    stencil[384:512, :] = jnp.where(rp == cz, bias(rj + 16 - cy), 0.0).astype(BF16)
    zat = jnp.where(iz == 0, 16, -2)
    stencil[512:640, :] = jnp.where(rp == cy, bias(rj + zat - cz), 0.0).astype(BF16)

    for copy in small:
        copy.wait()

    for i in range(CUBE):
        line = potv[0:1, PLANE * i : PLANE * (i + 1)]
        pterm[16 * i : 16 * i + 16, :] = jnp.broadcast_to(0.25 * (line - 2.25), (16, PLANE))

    for a in range(4):
        where = ptv[a : a + 1, :]
        upper, lower = where >> 7, where & 127
        hot = jnp.where(iota((128, 256), 0) == lower, one, nil).astype(BF16)
        values = projv[a]
        spread = jnp.concatenate(
            [jnp.where(upper == h, values, nil) for h in range(32)], axis=0
        )
        s0, rest = split(spread)
        s1, s2 = split(spread - s0.astype(F32))
        dense = dot(s0, hot, 1, 1) + (dot(s1, hot, 1, 1) + dot(s2, hot, 1, 1))
        flat = jnp.concatenate([dense[8 * h : 8 * h + 8, :] for h in range(32)], axis=1)
        mixed = lax.dot_general(
            0.25 * coupv[a], flat, (((0,), (0,)), ((), ())),
            preferred_element_type=F32, precision=lax.Precision.HIGHEST,
        )
        fh, fl = split(flat)
        eh, el = split(mixed)
        bhl[8 * a : 8 * a + 8, :] = fh.astype(F32)
        bhl[32 + 8 * a : 40 + 8 * a, :] = fl.astype(F32)
        ecat[8 * a : 8 * a + 8, :] = eh.astype(F32)
        ecat[32 + 8 * a : 40 + 8 * a, :] = eh.astype(F32)
        ecat[64 + 8 * a : 72 + 8 * a, :] = el.astype(F32)

    vx1[32:288, :] = inside(vx0) + outside(0, vx0)
    send_faces(1, vx1, (3, 4))
    pack_faces(1, vx1)
    send_faces(1, vx1, range(3))
    fs[...] = 2.0 * (inside(vx1) + outside(1, vx1)) - vx0[32:288, :]

    def to_piece(peer):
        return pltpu.make_async_remote_copy(
            src_ref=fs.at[pl.ds(pl.multiple_of(peer * 16, 16), 16), :],
            dst_ref=work.at[pl.ds(pl.multiple_of(band * 16, 16), 16), pl.ds(PLANE, PLANE)],
            send_sem=a_send.at[peer], recv_sem=a_recv.at[band],
            device_id=(dom, peer), device_id_type=MESH,
        )

    def from_piece(peer):
        return pltpu.make_async_remote_copy(
            src_ref=fs.at[pl.ds(0, 16), :],
            dst_ref=work.at[pl.ds(pl.multiple_of(peer * 16, 16), 16), pl.ds(PLANE, PLANE)],
            send_sem=a_send.at[peer], recv_sem=a_recv.at[peer],
            device_id=(dom, peer), device_id_type=MESH,
        )

    def peers(count, me, action):
        @pl.loop(0, count - 1)
        def _(k):
            step = count // 2 + (1 - 2 * lax.rem(k, 2)) * ((k + 1) // 2)
            action(lax.rem(me + step, count))

    peers(NBAND, band, lambda peer: to_piece(peer).start())
    mine = pl.ds(pl.multiple_of(band * 16, 16), 16)
    work[mine, PLANE : 2 * PLANE] = fs[mine, :]
    peers(NBAND, band, lambda peer: from_piece(peer).wait_recv())

    piece = work[:, PLANE : 2 * PLANE]
    ph, plo = split(piece)
    gram = (1.0 / POINTS) * (dot(ph, ph, 1, 1) + (dot(ph, plo, 1, 1) + dot(plo, ph, 1, 1)))
    row, col = iota((128, 128), 0), iota((128, 128), 1)
    low = gram[128:256, 128:256]
    packed = jnp.where(row >= col, gram[0:128, 0:128], low)
    diag = jnp.sum(jnp.where(row == col, low, 0.0), axis=0, keepdims=True)
    for c in range(NSET):
        part[c, 0:16, :] = packed[16 * c : 16 * c + 16, :]
        part[c, 16:32, :] = gram[128 + 16 * c : 144 + 16 * c, 0:128]
        part[c, 32:33, :] = diag

    def chunk(src, dst, send, recv, where):
        return pltpu.make_async_remote_copy(
            src_ref=src, dst_ref=dst, send_sem=send, recv_sem=recv, device_id=where, device_id_type=MESH
        )

    def share(count, me, at, buf, send, recv):
        peers(count, me, lambda peer: chunk(
            buf.at[me], buf.at[me], send.at[peer], recv.at[me], at(peer)).start())

    def collect(count, me, at, buf, send, recv):
        peers(count, me, lambda peer: chunk(
            buf.at[me], buf.at[peer], send.at[peer], recv.at[peer], at(peer)).wait_recv())

    def drain(count, me, at, buf, send, recv):
        peers(count, me, lambda peer: chunk(
            buf.at[me], buf.at[peer], send.at[peer], recv.at[peer], at(peer)).wait_send())

    def total(buf, count):
        value = buf[0]
        for i in range(1, count):
            value = value + buf[i]
        return value

    peers(NSET, mine_set, lambda peer: chunk(
        part.at[peer], rs_buf.at[mine_set], r_send.at[peer], r_recv.at[mine_set], at_set(peer)).start())
    rs_buf[mine_set] = part[mine_set]
    peers(NSET, mine_set, lambda peer: chunk(
        part.at[peer], rs_buf.at[peer], r_send.at[peer], r_recv.at[peer], at_set(peer)).wait_recv())
    value = total(rs_buf, NSET)
    a_y = (NY, py, at_y, ay_buf, s_send.at[0], s_recv.at[0])
    b_z = (NZ, pz, at_z, bz_buf, s_send.at[1], s_recv.at[1])
    a_z = (NZ, pz, at_z, az_buf, s_send.at[2], s_recv.at[2])
    b_y = (NY, py, at_y, by_buf, s_send.at[3], s_recv.at[3])
    a_set = (NSET, mine_set, at_set, g_buf, s_send.at[4], s_recv.at[4])
    ay_buf[py] = value[0:16]
    share(*a_y)
    bz_buf[pz] = value[16:33]
    share(*b_z)
    collect(*a_y)
    az_buf[pz] = total(ay_buf, NY)
    share(*a_z)
    collect(*b_z)
    by_buf[py] = total(bz_buf, NZ)
    share(*b_y)
    collect(*a_z)
    g_buf[mine_set, 0:16, :] = total(az_buf, NZ)
    collect(*b_y)
    g_buf[mine_set, 16:33, :] = total(by_buf, NY)
    share(*a_set)
    collect(*a_set)

    packed = jnp.concatenate([g_buf[c, 0:16, :] for c in range(NSET)], axis=0)
    cross = jnp.concatenate([g_buf[c, 16:32, :] for c in range(NSET)], axis=0)
    diag = jnp.broadcast_to(g_buf[0, 32:33, :], (128, 128))
    turned = packed.T
    work[0:128, 0:128] = jnp.where(row >= col, packed, turned)
    work[128:256, 128:256] = jnp.where(row < col, packed, jnp.where(row == col, diag, turned))
    work[128:256, 0:128] = cross
    work[0:128, 128:256] = cross.T

    def to_out(peer):
        return pltpu.make_async_remote_copy(
            src_ref=fs.at[pl.ds(pl.multiple_of(peer * 16, 16), 16), :],
            dst_ref=out.at[:, pl.ds(pl.multiple_of(band * PLANE, PLANE), PLANE)],
            send_sem=o_send.at[peer], recv_sem=o_recv.at[band],
            device_id=(dom, peer), device_id_type=MESH,
        )

    def from_out(peer):
        return pltpu.make_async_remote_copy(
            src_ref=fs.at[pl.ds(0, 16), :],
            dst_ref=out.at[:, pl.ds(pl.multiple_of(peer * PLANE, PLANE), PLANE)],
            send_sem=o_send.at[peer], recv_sem=o_recv.at[peer],
            device_id=(dom, peer), device_id_type=MESH,
        )

    peers(NBAND, band, lambda peer: to_piece(peer).wait_send())

    srow = iota((8, 128), 0)

    def spread_row(value, k):
        return jnp.broadcast_to(value[k : k + 1, :], (8, 128))

    for j in range(256 // BLOCK):
        first = j * BLOCK
        lo = first // 128 * 128
        count = BLOCK // 8
        tiles = [
            [work[first + 8 * t : first + 8 * t + 8, c : c + 128] for c in range(lo, 512, 128)]
            for t in range(count)
        ]
        for s in range(count):
            at = first - lo + 8 * s
            cols = {
                t: [jnp.broadcast_to(tiles[t][0][:, at + k : at + k + 1], (8, 128)) for k in range(8)]
                for t in range(s, count)
            }
            pivots = cols[s][0]
            for k in range(8):
                inverse = 1.0 / spread_row(cols[s][k], k)
                pivots = jnp.where(srow == k, cols[s][k], pivots)
                heads = {m: spread_row(cols[s][m], k) for m in range(k + 1, 8)}
                lead = [spread_row(v, k) for v in tiles[s]]
                for t in range(s, count):
                    if t == s and k == 7:
                        continue
                    factor = cols[t][k] * inverse
                    if t == s:
                        factor = jnp.where(srow > k, factor, 0.0)
                    for m in range(k + 1, 8):
                        cols[t][m] = cols[t][m] - factor * heads[m]
                    tiles[t] = [v - factor * r for v, r in zip(tiles[t], lead)]
            scale = lax.rsqrt(pivots)
            tiles[s] = [v * scale for v in tiles[s]]
        lanes = [jnp.concatenate([tiles[t][c] for t in range(count)], axis=0) for c in range((512 - lo) // 128)]
        fs[first : first + BLOCK, 0:128] = lanes[-2]
        fs[first : first + BLOCK, 128:256] = lanes[-1]
        for half in range(BLOCK // 16):
            peer = j * (BLOCK // 16) + half

            @pl.when(peer != band)
            def _():
                to_out(peer).start()

        after = first + BLOCK
        if after < 256:
            base = after // 128 * 128
            rest = jnp.concatenate(lanes[(base - lo) // 128 :], axis=1)
            high, low = split(rest)
            lead = high[:, 0 : 256 - base].astype(F32)
            left = jnp.concatenate([lead, lead, rest[:, 0 : 256 - base] - lead], axis=0).T
            left = left[after - base :, :].astype(BF16)
            work[after:256, base:512] = work[after:256, base:512] - dot(
                left, jnp.concatenate([high, low, high], axis=0)
            )

    own = pltpu.make_async_copy(
        fs.at[mine, :], out.at[:, pl.ds(pl.multiple_of(band * PLANE, PLANE), PLANE)], o_own
    )
    own.start()
    for turn, ref in ((0, vx0), (1, vx1)):
        for face in halo(turn, ref):
            under(face[0], face[2].wait_send)
    peers(NSET, mine_set, lambda peer: chunk(
        part.at[peer], rs_buf.at[peer], r_send.at[peer], r_recv.at[peer], at_set(peer)).wait_send())
    for stage in (a_y, b_z, a_z, b_y, a_set):
        drain(*stage)
    peers(NBAND, band, lambda peer: from_out(peer).wait_recv())
    peers(NBAND, band, lambda peer: to_out(peer).wait_send())
    own.wait()


def local(waves, potential, atom_points, projectors, coupling):
    dma = pltpu.SemaphoreType.DMA
    vmem = pltpu.VMEM
    return pl.pallas_call(
        kernel,
        out_shape=jax.ShapeDtypeStruct((BAND_LOC, CUBE**3), F32),
        in_specs=[pl.BlockSpec(memory_space=pl.ANY)] * 5,
        out_specs=pl.BlockSpec(memory_space=pl.ANY),
        scratch_shapes=[
            vmem((320, 256), F32), vmem((320, 256), F32), vmem((256, 256), F32),
            vmem((2, 3, 64, 128), F32), vmem((2, 3, 64, 128), F32),
            vmem((256, 384), BF16), vmem((640, 256), BF16),
            vmem((64, 4096), F32), vmem((96, 4096), F32),
            vmem((256, 256), F32), vmem((256, 512), F32),
            vmem((4, 256), jnp.int32), vmem((4, 8, 256), F32), vmem((4, 8, 8), F32), vmem((1, 4096), F32),
            vmem((NSET, ROWS, 128), F32), vmem((NSET, ROWS, 128), F32),
            vmem((NY, 16, 128), F32), vmem((NZ, 16, 128), F32),
            vmem((NZ, 17, 128), F32), vmem((NY, 17, 128), F32), vmem((NSET, ROWS, 128), F32),
            dma((20,)), dma((2, 5)), dma((2, 5)), dma((16,)), dma((16,)), dma((8,)), dma((8,)),
            dma((5, 8)), dma((5, 8)), dma((16,)), dma((16,)), dma,
        ],
        compiler_params=pltpu.CompilerParams(collective_id=0, has_side_effects=True),
    )(waves, potential.reshape(1, CUBE**3), atom_points, projectors, coupling)


def solution(mesh):
    placed = (
        P("band", "dom"),
        P("dom"),
        P("dom", None),
        P("dom", None, None),
        P("dom", None, None),
    )
    return jax.shard_map(
        local, mesh=mesh, in_specs=placed, out_specs=P("band", "dom"), check_vma=False
    )
```

```python
import jax
import jax.numpy as jnp
from jax import lax
from jax.experimental import pallas as pl
from jax.experimental.pallas import tpu as pltpu
from jax.sharding import PartitionSpec as P

F32, BF16 = jnp.float32, jnp.bfloat16
MESH = pl.DeviceIdType.MESH
CUBE = 16
BAND_LOC = 16
PLANE = CUBE * CUBE
POINTS = 131072
NBAND, NZ, NY, NX, NSET = 16, 8, 8, 4, 8
ROWS = 33
BLOCK = 32


def iota(shape, dim):
    return lax.broadcasted_iota(jnp.int32, shape, dim)


def split(x):
    big = x.astype(BF16)
    return big, (x - big.astype(F32)).astype(BF16)


def dot(a, b, ca=1, cb=0):
    return lax.dot_general(a, b, (((ca,), (cb,)), ((), ())), preferred_element_type=F32)


def bias(delta):
    step = jnp.abs(delta)
    return jnp.where(step == 1, -16.0, jnp.where(step == 2, 1.0, 0.0))


def kernel(
    waves, pot, pts, proj, coup, out,
    vx0, vx1, pterm, facesend, facerecv, pick, stencil, bcat, couple, fs, work,
    ptv, projv, coupv, potv, part, rs_buf, ay_buf, az_buf, bz_buf, by_buf, g_buf,
    in_sem, h_send, h_recv, a_send, a_recv, r_send, r_recv, s_send, s_recv, o_send, o_recv, o_own,
):
    dom, band = lax.axis_index("dom"), lax.axis_index("band")
    pz, px = dom // NX, lax.rem(dom, NX)
    py, core = band // 2, lax.rem(band, 2)
    mine_set = px * 2 + core
    iz = lax.rem(dom, 2)
    iy = lax.rem(dom // 2, 4)
    ix = dom // 8
    middle = jnp.logical_or(iy == 1, iy == 2)

    copies = [
        pltpu.make_async_copy(
            waves.at[:, pl.ds(PLANE * i, PLANE)], vx0.at[pl.ds(32 + 16 * i, 16), :], in_sem.at[i]
        )
        for i in range(CUBE)
    ]
    small = [
        pltpu.make_async_copy(src, dst, in_sem.at[16 + i])
        for i, (src, dst) in enumerate(((pts, ptv), (proj, projv), (coup, coupv), (pot, potv)))
    ]
    for copy in copies + small:
        copy.start()

    facerecv[...] = jnp.zeros_like(facerecv)
    couple[...] = jnp.zeros_like(couple)
    for ref in (vx0, vx1):
        ref[0:32, :] = jnp.zeros((32, PLANE), F32)
        ref[288:320, :] = jnp.zeros((32, PLANE), F32)

    def at_band(peer):
        return (dom, peer)

    def at_y(peer):
        return (dom, peer * 2 + core)

    def at_z(peer):
        return (peer * NX + px, band)

    def at_set(peer):
        return (pz * NX + peer // 2, py * 2 + lax.rem(peer, 2))

    barrier = pltpu.get_barrier_semaphore()

    def greet(where):
        pl.semaphore_signal(barrier, inc=1, device_id=where, device_id_type=MESH)

    @pl.loop(1, NBAND)
    def _(k):
        greet((dom, lax.rem(band + k, NBAND)))

    @pl.loop(1, NZ)
    def _(k):
        greet((lax.rem(pz + k, NZ) * NX + px, band))

    @pl.loop(1, NSET)
    def _(k):
        greet(at_set(lax.rem(mine_set + k, NSET)))

    @pl.when(iy == 1)
    def _():
        greet((dom + 2, band))

    @pl.when(iy == 2)
    def _():
        greet((dom - 2, band))

    group = iota((64, 128), 1) >> 5

    def halo(turn, ref):
        def face(slot, src, dst, where):
            return pltpu.make_async_remote_copy(
                src_ref=src, dst_ref=dst, send_sem=h_send.at[turn, slot],
                recv_sem=h_recv.at[turn, slot], device_id=(where, band), device_id_type=MESH,
            )
        return (
            (iy > 0, iy < 3, face(0, facesend.at[turn, 0], facerecv.at[turn, 1], dom - 2)),
            (iy < 3, iy > 0, face(1, facesend.at[turn, 1], facerecv.at[turn, 0], dom + 2)),
            (None, None, face(2, facesend.at[turn, 2], facerecv.at[turn, 2], dom + 1 - 2 * iz)),
            (ix > 0, ix < 3, face(3, ref.at[pl.ds(32, 32), :], ref.at[pl.ds(288, 32), :], dom - 8)),
            (ix < 3, ix > 0, face(4, ref.at[pl.ds(256, 32), :], ref.at[pl.ds(0, 32), :], dom + 8)),
        )

    def under(condition, action):
        if condition is None:
            action()
        else:
            pl.when(condition)(action)

    def pack_y(turn, ref):
        for slot, at in ((0, 0), (1, 128)):
            packed = None
            for g in range(4):
                shift = (32 * g + 32 * slot) % 128
                part = ref[32 + 64 * g : 96 + 64 * g, at : at + 128]
                part = pltpu.roll(part, shift, 1) if shift else part
                packed = part if g == 0 else jnp.where(group == g, part, packed)
            facesend[turn, slot] = packed

    def pack_z(turn, ref):
        vh, vl = split(ref[32:288, :])
        ends = dot(vh, pick[...]) + dot(vl, pick[...])
        packed = ends[0:64, :]
        for g in range(1, 4):
            packed = jnp.where(group == g, ends[64 * g : 64 * g + 64, :], packed)
        facesend[turn, 2] = packed

    def send_faces(turn, ref, slots):
        faces = halo(turn, ref)
        for slot in slots:
            under(faces[slot][0], faces[slot][2].start)

    def inside(ref):
        here = ref[32:288, :]
        vh, vl = split(here)
        both = jnp.concatenate(
            [jnp.concatenate([v[16 * i : 16 * i + 16, :] for i in range(CUBE)], axis=1) for v in (vh, vl)],
            axis=0,
        )
        quad = dot(both, bcat[0:64, :], 1, 1)
        coef = quad[0:16, 0:32] + (quad[0:16, 32:64] + quad[16:32, 0:32])
        ch, cl = split(coef)
        kh, kl = split(couple[...])
        ch, cl = split(dot(ch, kh, 1, 1) + (dot(ch, kl, 1, 1) + dot(cl, kh, 1, 1)))
        added = dot(jnp.concatenate([ch, ch, cl], axis=1), bcat[...])
        added = jnp.concatenate([added[:, PLANE * i : PLANE * (i + 1)] for i in range(CUBE)], axis=0)
        inner = dot(vh, stencil[0:256, :]) + dot(vl, stencil[0:256, :])
        return pterm[...] * here + added + (1.0 / 96.0) * inner

    def outside(turn, ref):
        for face in halo(turn, ref):
            under(face[1], face[2].wait_recv)
        wide = jnp.concatenate(
            [
                jnp.concatenate(
                    [jnp.where(group == g, facerecv[turn, slot], 0.0) for g in range(4)], axis=0
                )
                for slot in range(3)
            ],
            axis=1,
        )
        wh, wl = split(wide)
        outer = dot(wh, stencil[256:640, :]) + dot(wl, stencil[256:640, :])
        far = ref[0:256, :] + ref[64:320, :]
        near = ref[16:272, :] + ref[48:304, :]
        return (1.0 / 96.0) * (outer + (far - 16.0 * near))

    row, col = iota((PLANE, 128), 0), iota((PLANE, 128), 1)
    ry, rz = row >> 4, row & 15
    cj, cp = (col >> 4) & 1, col & 15
    one, nil = jnp.float32(1), jnp.float32(0)
    zlo = jnp.where(iz == 0, 14, 0)
    pick[...] = jnp.where(row == cp * 16 + cj + zlo, one, nil).astype(BF16)

    for copy in copies:
        copy.wait()
    pack_y(0, vx0)
    pack_z(0, vx0)
    pl.semaphore_wait(barrier, 29 + middle.astype(jnp.int32))
    send_faces(0, vx0, range(5))

    row, col = iota((PLANE, PLANE), 0), iota((PLANE, PLANE), 1)
    ry, rz, cy, cz = row >> 4, row & 15, col >> 4, col & 15
    stencil[0:256, :] = (
        jnp.where(rz == cz, bias(ry - cy), 0.0) + jnp.where(ry == cy, bias(rz - cz), 0.0)
    ).astype(BF16)
    row, col = iota((128, PLANE), 0), iota((128, PLANE), 1)
    cy, cz = col >> 4, col & 15
    rj, rp = (row >> 4) & 1, row & 15
    stencil[256:384, :] = jnp.where(rp == cz, bias(rj - 2 - cy), 0.0).astype(BF16)
    stencil[384:512, :] = jnp.where(rp == cz, bias(rj + 16 - cy), 0.0).astype(BF16)
    zat = jnp.where(iz == 0, 16, -2)
    stencil[512:640, :] = jnp.where(rp == cy, bias(rj + zat - cz), 0.0).astype(BF16)

    for copy in small:
        copy.wait()

    for i in range(CUBE):
        line = potv[0:1, PLANE * i : PLANE * (i + 1)]
        pterm[16 * i : 16 * i + 16, :] = jnp.broadcast_to(0.25 * (line - 2.25), (16, PLANE))

    for pair in range(2):
        flats = []
        for a in (2 * pair, 2 * pair + 1):
            where = ptv[a : a + 1, :]
            upper, lower = where >> 7, where & 127
            hot = jnp.where(iota((128, 256), 0) == lower, one, nil).astype(BF16)
            values = projv[a]
            lead = values.astype(BF16).astype(F32)
            parts = jnp.concatenate([lead, values - lead], axis=0)
            spread = jnp.concatenate(
                [jnp.where(upper == h, parts, nil).astype(BF16) for h in range(32)], axis=0
            )
            dense = dot(spread, hot, 1, 1)
            flats.append(
                [dense[16 * h : 16 * h + 8, :] + dense[16 * h + 8 : 16 * h + 16, :] for h in range(32)]
            )
            couple[8 * a : 8 * a + 8, 8 * a : 8 * a + 8] = 0.25 * coupv[a]
        for h in range(32):
            fh, fl = split(jnp.concatenate([flats[0][h], flats[1][h]], axis=0))
            here = slice(128 * h, 128 * h + 128)
            bcat[16 * pair : 16 * pair + 16, here] = fh
            bcat[32 + 16 * pair : 48 + 16 * pair, here] = fl
            bcat[64 + 16 * pair : 80 + 16 * pair, here] = fh

    vx1[32:288, :] = inside(vx0) + outside(0, vx0)
    send_faces(1, vx1, (3, 4))
    pack_y(1, vx1)
    send_faces(1, vx1, (0, 1))
    pack_z(1, vx1)
    send_faces(1, vx1, (2,))
    fs[...] = 2.0 * (inside(vx1) + outside(1, vx1)) - vx0[32:288, :]

    def to_piece(peer):
        return pltpu.make_async_remote_copy(
            src_ref=fs.at[pl.ds(pl.multiple_of(peer * 16, 16), 16), :],
            dst_ref=work.at[pl.ds(pl.multiple_of(band * 16, 16), 16), pl.ds(PLANE, PLANE)],
            send_sem=a_send.at[peer], recv_sem=a_recv.at[band],
            device_id=(dom, peer), device_id_type=MESH,
        )

    def from_piece(peer):
        return pltpu.make_async_remote_copy(
            src_ref=fs.at[pl.ds(0, 16), :],
            dst_ref=work.at[pl.ds(pl.multiple_of(peer * 16, 16), 16), pl.ds(PLANE, PLANE)],
            send_sem=a_send.at[peer], recv_sem=a_recv.at[peer],
            device_id=(dom, peer), device_id_type=MESH,
        )

    def peers(count, me, action):
        @pl.loop(0, count - 1)
        def _(k):
            step = count // 2 + (1 - 2 * lax.rem(k, 2)) * ((k + 1) // 2)
            action(lax.rem(me + step, count))

    peers(NBAND, band, lambda peer: to_piece(peer).start())
    mine = pl.ds(pl.multiple_of(band * 16, 16), 16)
    work[mine, PLANE : 2 * PLANE] = fs[mine, :]
    peers(NBAND, band, lambda peer: from_piece(peer).wait_recv())

    piece = work[:, PLANE : 2 * PLANE]
    ph, plo = split(piece)
    gram = (1.0 / POINTS) * (dot(ph, ph, 1, 1) + (dot(ph, plo, 1, 1) + dot(plo, ph, 1, 1)))
    row, col = iota((128, 128), 0), iota((128, 128), 1)
    low = gram[128:256, 128:256]
    packed = jnp.where(row >= col, gram[0:128, 0:128], low)
    diag = jnp.sum(jnp.where(row == col, low, 0.0), axis=0, keepdims=True)
    for c in range(NSET):
        part[c, 0:16, :] = packed[16 * c : 16 * c + 16, :]
        part[c, 16:32, :] = gram[128 + 16 * c : 144 + 16 * c, 0:128]
        part[c, 32:33, :] = diag

    def chunk(src, dst, send, recv, where):
        return pltpu.make_async_remote_copy(
            src_ref=src, dst_ref=dst, send_sem=send, recv_sem=recv, device_id=where, device_id_type=MESH
        )

    def share(count, me, at, buf, send, recv):
        peers(count, me, lambda peer: chunk(
            buf.at[me], buf.at[me], send.at[peer], recv.at[me], at(peer)).start())

    def collect(count, me, at, buf, send, recv):
        peers(count, me, lambda peer: chunk(
            buf.at[me], buf.at[peer], send.at[peer], recv.at[peer], at(peer)).wait_recv())

    def drain(count, me, at, buf, send, recv):
        peers(count, me, lambda peer: chunk(
            buf.at[me], buf.at[peer], send.at[peer], recv.at[peer], at(peer)).wait_send())

    def total(buf, count):
        value = buf[0]
        for i in range(1, count):
            value = value + buf[i]
        return value

    peers(NSET, mine_set, lambda peer: chunk(
        part.at[peer], rs_buf.at[mine_set], r_send.at[peer], r_recv.at[mine_set], at_set(peer)).start())
    rs_buf[mine_set] = part[mine_set]
    peers(NSET, mine_set, lambda peer: chunk(
        part.at[peer], rs_buf.at[peer], r_send.at[peer], r_recv.at[peer], at_set(peer)).wait_recv())
    value = total(rs_buf, NSET)
    a_y = (NY, py, at_y, ay_buf, s_send.at[0], s_recv.at[0])
    b_z = (NZ, pz, at_z, bz_buf, s_send.at[1], s_recv.at[1])
    a_z = (NZ, pz, at_z, az_buf, s_send.at[2], s_recv.at[2])
    b_y = (NY, py, at_y, by_buf, s_send.at[3], s_recv.at[3])
    a_set = (NSET, mine_set, at_set, g_buf, s_send.at[4], s_recv.at[4])
    ay_buf[py] = value[0:16]
    share(*a_y)
    bz_buf[pz] = value[16:33]
    share(*b_z)
    collect(*a_y)
    az_buf[pz] = total(ay_buf, NY)
    share(*a_z)
    collect(*b_z)
    by_buf[py] = total(bz_buf, NZ)
    share(*b_y)
    collect(*a_z)
    g_buf[mine_set, 0:16, :] = total(az_buf, NZ)
    collect(*b_y)
    g_buf[mine_set, 16:33, :] = total(by_buf, NY)
    share(*a_set)
    collect(*a_set)

    packed = jnp.concatenate([g_buf[c, 0:16, :] for c in range(NSET)], axis=0)
    cross = jnp.concatenate([g_buf[c, 16:32, :] for c in range(NSET)], axis=0)
    diag = jnp.broadcast_to(g_buf[0, 32:33, :], (128, 128))
    turned = packed.T
    work[0:128, 0:128] = jnp.where(row >= col, packed, turned)
    work[128:256, 128:256] = jnp.where(row < col, packed, jnp.where(row == col, diag, turned))
    work[128:256, 0:128] = cross
    work[0:128, 128:256] = cross.T

    def to_out(peer):
        return pltpu.make_async_remote_copy(
            src_ref=fs.at[pl.ds(pl.multiple_of(peer * 16, 16), 16), :],
            dst_ref=out.at[:, pl.ds(pl.multiple_of(band * PLANE, PLANE), PLANE)],
            send_sem=o_send.at[peer], recv_sem=o_recv.at[band],
            device_id=(dom, peer), device_id_type=MESH,
        )

    def from_out(peer):
        return pltpu.make_async_remote_copy(
            src_ref=fs.at[pl.ds(0, 16), :],
            dst_ref=out.at[:, pl.ds(pl.multiple_of(peer * PLANE, PLANE), PLANE)],
            send_sem=o_send.at[peer], recv_sem=o_recv.at[peer],
            device_id=(dom, peer), device_id_type=MESH,
        )

    peers(NBAND, band, lambda peer: to_piece(peer).wait_send())

    srow = iota((8, 128), 0)

    def spread_row(value, k):
        return jnp.broadcast_to(value[k : k + 1, :], (8, 128))

    for j in range(256 // BLOCK):
        first = j * BLOCK
        lo = first // 128 * 128
        count = BLOCK // 8
        tiles = [
            [work[first + 8 * t : first + 8 * t + 8, c : c + 128] for c in range(lo, 512, 128)]
            for t in range(count)
        ]

        def columns(s, start):
            at = first - lo + 8 * s
            return {
                t: [jnp.broadcast_to(tiles[t][0][:, at + k : at + k + 1], (8, 128)) for k in range(8)]
                for t in range(start, count)
            }

        cols = columns(0, 0)
        for s in range(count):
            coming = columns(s + 1, s) if s + 1 < count else None
            factors = []
            pivot = spread_row(cols[s][0], 0)
            pivots = pivot
            for k in range(8):
                inverse = 1.0 / pivot
                heads = {m: spread_row(cols[s][m], k) for m in range(k + 1, 8)}
                lead = [spread_row(v, k) for v in tiles[s]]
                if k < 7:
                    pivot = spread_row(cols[s][k + 1], k + 1) - (
                        spread_row(cols[s][k], k + 1) * inverse
                    ) * heads[k + 1]
                    pivots = jnp.where(srow > k, pivot, pivots)
                factor = {
                    t: (jnp.where(srow > k, cols[s][k], 0.0) if t == s else cols[t][k]) * inverse
                    for t in range(s, count)
                    if t != s or k < 7
                }
                factors.append(factor)
                for t in factor:
                    for m in range(k + 1, 8):
                        cols[t][m] = cols[t][m] - factor[t] * heads[m]
                    tiles[t] = [v - factor[t] * r for v, r in zip(tiles[t], lead)]
            if coming is not None:
                for k in range(8):
                    heads = [spread_row(coming[s][m], k) for m in range(8)]
                    for t in factors[k]:
                        for m in range(8):
                            coming[t][m] = coming[t][m] - factors[k][t] * heads[m]
                cols = coming
            scale = lax.rsqrt(pivots)
            tiles[s] = [v * scale for v in tiles[s]]
        lanes = [jnp.concatenate([tiles[t][c] for t in range(count)], axis=0) for c in range((512 - lo) // 128)]
        fs[first : first + BLOCK, 0:128] = lanes[-2]
        fs[first : first + BLOCK, 128:256] = lanes[-1]
        for half in range(BLOCK // 16):
            peer = j * (BLOCK // 16) + half

            @pl.when(peer != band)
            def _():
                to_out(peer).start()

        after = first + BLOCK
        if after < 256:
            base = after // 128 * 128
            rest = jnp.concatenate(lanes[(base - lo) // 128 :], axis=1)
            high, low = split(rest)
            lead = high[:, 0 : 256 - base].astype(F32)
            left = jnp.concatenate([lead, lead, rest[:, 0 : 256 - base] - lead], axis=0).T
            left = left[after - base :, :].astype(BF16)
            work[after:256, base:512] = work[after:256, base:512] - dot(
                left, jnp.concatenate([high, low, high], axis=0)
            )

    own = pltpu.make_async_copy(
        fs.at[mine, :], out.at[:, pl.ds(pl.multiple_of(band * PLANE, PLANE), PLANE)], o_own
    )
    own.start()
    for turn, ref in ((0, vx0), (1, vx1)):
        for face in halo(turn, ref):
            under(face[0], face[2].wait_send)
    peers(NSET, mine_set, lambda peer: chunk(
        part.at[peer], rs_buf.at[peer], r_send.at[peer], r_recv.at[peer], at_set(peer)).wait_send())
    for stage in (a_y, b_z, a_z, b_y, a_set):
        drain(*stage)
    peers(NBAND, band, lambda peer: from_out(peer).wait_recv())
    peers(NBAND, band, lambda peer: to_out(peer).wait_send())
    own.wait()


def local(waves, potential, atom_points, projectors, coupling):
    dma = pltpu.SemaphoreType.DMA
    vmem = pltpu.VMEM
    return pl.pallas_call(
        kernel,
        out_shape=jax.ShapeDtypeStruct((BAND_LOC, CUBE**3), F32),
        in_specs=[pl.BlockSpec(memory_space=pltpu.MemorySpace.HBM)] * 5,
        out_specs=pl.BlockSpec(memory_space=pl.ANY),
        scratch_shapes=[
            vmem((320, 256), F32), vmem((320, 256), F32), vmem((256, 256), F32),
            vmem((2, 3, 64, 128), F32), vmem((2, 3, 64, 128), F32),
            vmem((256, 128), BF16), vmem((640, 256), BF16),
            vmem((96, 4096), BF16), vmem((32, 32), F32),
            vmem((256, 256), F32), vmem((256, 512), F32),
            vmem((4, 256), jnp.int32), vmem((4, 8, 256), F32), vmem((4, 8, 8), F32), vmem((1, 4096), F32),
            vmem((NSET, ROWS, 128), F32), vmem((NSET, ROWS, 128), F32),
            vmem((NY, 16, 128), F32), vmem((NZ, 16, 128), F32),
            vmem((NZ, 17, 128), F32), vmem((NY, 17, 128), F32), vmem((NSET, ROWS, 128), F32),
            dma((20,)), dma((2, 5)), dma((2, 5)), dma((16,)), dma((16,)), dma((8,)), dma((8,)),
            dma((5, 8)), dma((5, 8)), dma((16,)), dma((16,)), dma,
        ],
        compiler_params=pltpu.CompilerParams(collective_id=0, has_side_effects=True, vmem_limit_bytes=12 << 20),
    )(
        *(
            pltpu.with_memory_space_constraint(value, pltpu.MemorySpace.HBM)
            for value in (waves, potential.reshape(1, CUBE**3), atom_points, projectors, coupling)
        )
    )


def solution(mesh):
    placed = (
        P("band", "dom"),
        P("dom"),
        P("dom", None),
        P("dom", None, None),
        P("dom", None, None),
    )
    return jax.shard_map(
        local, mesh=mesh, in_specs=placed, out_specs=P("band", "dom"), check_vma=False
    )
```

```python
import jax
import jax.numpy as jnp
from jax import lax
from jax.experimental import pallas as pl
from jax.experimental.pallas import tpu as pltpu
from jax.sharding import PartitionSpec as P

F32, BF16 = jnp.float32, jnp.bfloat16
MESH = pl.DeviceIdType.MESH
CUBE = 16
BAND_LOC = 16
PLANE = CUBE * CUBE
POINTS = 131072
NBAND, NZ, NY, NX, NSET = 16, 8, 8, 4, 8
ROWS = 33
BLOCK = 32


def iota(shape, dim):
    return lax.broadcasted_iota(jnp.int32, shape, dim)


def split(x):
    big = x.astype(BF16)
    return big, (x - big.astype(F32)).astype(BF16)


def dot(a, b, ca=1, cb=0):
    return lax.dot_general(a, b, (((ca,), (cb,)), ((), ())), preferred_element_type=F32)


def bias(delta):
    step = jnp.abs(delta)
    return jnp.where(step == 1, -16.0, jnp.where(step == 2, 1.0, 0.0))


def kernel(
    waves, pot, pts, proj, coup, out,
    vx0, vx1, pterm, facesend, facerecv, pick, stencil, bcat, couple, fs, work,
    ptv, projv, coupv, potv, part, rs_buf, ay_buf, az_buf, bz_buf, by_buf, g_buf,
    in_sem, h_send, h_recv, a_send, a_recv, r_send, r_recv, s_send, s_recv, o_send, o_recv, o_own,
):
    dom, band = lax.axis_index("dom"), lax.axis_index("band")
    pz, px = dom // NX, lax.rem(dom, NX)
    py, core = band // 2, lax.rem(band, 2)
    mine_set = px * 2 + core
    iz = lax.rem(dom, 2)
    iy = lax.rem(dom // 2, 4)
    ix = dom // 8
    middle = jnp.logical_or(iy == 1, iy == 2)

    copies = [
        pltpu.make_async_copy(
            waves.at[:, pl.ds(PLANE * i, PLANE)], vx0.at[pl.ds(32 + 16 * i, 16), :], in_sem.at[i]
        )
        for i in range(CUBE)
    ]
    small = [
        pltpu.make_async_copy(src, dst, in_sem.at[16 + i])
        for i, (src, dst) in enumerate(((pts, ptv), (proj, projv), (coup, coupv), (pot, potv)))
    ]
    for copy in copies + small:
        copy.start()

    facerecv[...] = jnp.zeros_like(facerecv)
    couple[...] = jnp.zeros_like(couple)
    for ref in (vx0, vx1):
        ref[0:32, :] = jnp.zeros((32, PLANE), F32)
        ref[288:320, :] = jnp.zeros((32, PLANE), F32)

    def at_band(peer):
        return (dom, peer)

    def at_y(peer):
        return (dom, peer * 2 + core)

    def at_z(peer):
        return (peer * NX + px, band)

    def at_set(peer):
        return (pz * NX + peer // 2, py * 2 + lax.rem(peer, 2))

    barrier = pltpu.get_barrier_semaphore()

    def greet(where):
        pl.semaphore_signal(barrier, inc=1, device_id=where, device_id_type=MESH)

    @pl.loop(1, NBAND)
    def _(k):
        greet((dom, lax.rem(band + k, NBAND)))

    @pl.loop(1, NZ)
    def _(k):
        greet((lax.rem(pz + k, NZ) * NX + px, band))

    @pl.loop(1, NSET)
    def _(k):
        greet(at_set(lax.rem(mine_set + k, NSET)))

    @pl.when(iy == 1)
    def _():
        greet((dom + 2, band))

    @pl.when(iy == 2)
    def _():
        greet((dom - 2, band))

    group = iota((64, 128), 1) >> 5

    def halo(turn, ref):
        def face(slot, src, dst, where):
            return pltpu.make_async_remote_copy(
                src_ref=src, dst_ref=dst, send_sem=h_send.at[turn, slot],
                recv_sem=h_recv.at[turn, slot], device_id=(where, band), device_id_type=MESH,
            )
        return (
            (iy > 0, iy < 3, face(0, facesend.at[turn, 0], facerecv.at[turn, 1], dom - 2)),
            (iy < 3, iy > 0, face(1, facesend.at[turn, 1], facerecv.at[turn, 0], dom + 2)),
            (None, None, face(2, facesend.at[turn, 2], facerecv.at[turn, 2], dom + 1 - 2 * iz)),
            (ix > 0, ix < 3, face(3, ref.at[pl.ds(32, 32), :], ref.at[pl.ds(288, 32), :], dom - 8)),
            (ix < 3, ix > 0, face(4, ref.at[pl.ds(256, 32), :], ref.at[pl.ds(0, 32), :], dom + 8)),
        )

    def under(condition, action):
        if condition is None:
            action()
        else:
            pl.when(condition)(action)

    def pack_y(turn, ref):
        for slot, at in ((0, 0), (1, 128)):
            packed = None
            for g in range(4):
                shift = (32 * g + 32 * slot) % 128
                part = ref[32 + 64 * g : 96 + 64 * g, at : at + 128]
                part = pltpu.roll(part, shift, 1) if shift else part
                packed = part if g == 0 else jnp.where(group == g, part, packed)
            facesend[turn, slot] = packed

    def pack_z(turn, ref):
        vh, vl = split(ref[32:288, :])
        ends = dot(vh, pick[...]) + dot(vl, pick[...])
        packed = ends[0:64, :]
        for g in range(1, 4):
            packed = jnp.where(group == g, ends[64 * g : 64 * g + 64, :], packed)
        facesend[turn, 2] = packed

    def send_faces(turn, ref, slots):
        faces = halo(turn, ref)
        for slot in slots:
            under(faces[slot][0], faces[slot][2].start)

    def inside(ref):
        here = ref[32:288, :]
        vh, vl = split(here)
        both = jnp.concatenate(
            [jnp.concatenate([v[16 * i : 16 * i + 16, :] for i in range(CUBE)], axis=1) for v in (vh, vl)],
            axis=0,
        )
        quad = dot(both, bcat[0:64, :], 1, 1)
        coef = quad[0:16, 0:32] + (quad[0:16, 32:64] + quad[16:32, 0:32])
        ch, cl = split(coef)
        kh, kl = split(couple[...])
        ch, cl = split(dot(ch, kh, 1, 1) + (dot(ch, kl, 1, 1) + dot(cl, kh, 1, 1)))
        added = dot(jnp.concatenate([ch, ch, cl], axis=1), bcat[...])
        added = jnp.concatenate([added[:, PLANE * i : PLANE * (i + 1)] for i in range(CUBE)], axis=0)
        inner = dot(vh, stencil[0:256, :]) + dot(vl, stencil[0:256, :])
        return pterm[...] * here + added + (1.0 / 96.0) * inner

    def from_faces(turn, slots):
        wide = jnp.concatenate(
            [
                jnp.concatenate(
                    [jnp.where(group == g, facerecv[turn, slot], 0.0) for g in range(4)], axis=0
                )
                for slot in slots
            ],
            axis=1,
        )
        wh, wl = split(wide)
        table = stencil[256 + 128 * slots[0] : 384 + 128 * slots[-1], :]
        return jnp.concatenate(
            [dot(wh[r : r + 128], table) + dot(wl[r : r + 128], table) for r in (0, 128)], axis=0
        )

    def outside(turn, ref):
        faces = halo(turn, ref)
        for slot in (2, 3, 4):
            under(faces[slot][1], faces[slot][2].wait_recv)
        far = ref[0:256, :] + ref[64:320, :]
        near = ref[16:272, :] + ref[48:304, :]
        value = from_faces(turn, (2,)) + (far - 16.0 * near)
        for slot in (0, 1):
            under(faces[slot][1], faces[slot][2].wait_recv)
        return (1.0 / 96.0) * (value + from_faces(turn, (0, 1)))

    row, col = iota((PLANE, 128), 0), iota((PLANE, 128), 1)
    ry, rz = row >> 4, row & 15
    cj, cp = (col >> 4) & 1, col & 15
    one, nil = jnp.float32(1), jnp.float32(0)
    zlo = jnp.where(iz == 0, 14, 0)
    pick[...] = jnp.where(row == cp * 16 + cj + zlo, one, nil).astype(BF16)

    for copy in copies:
        copy.wait()
    pack_y(0, vx0)
    pack_z(0, vx0)
    pl.semaphore_wait(barrier, 29 + middle.astype(jnp.int32))
    send_faces(0, vx0, range(5))

    row, col = iota((PLANE, PLANE), 0), iota((PLANE, PLANE), 1)
    ry, rz, cy, cz = row >> 4, row & 15, col >> 4, col & 15
    stencil[0:256, :] = (
        jnp.where(rz == cz, bias(ry - cy), 0.0) + jnp.where(ry == cy, bias(rz - cz), 0.0)
    ).astype(BF16)
    row, col = iota((128, PLANE), 0), iota((128, PLANE), 1)
    cy, cz = col >> 4, col & 15
    rj, rp = (row >> 4) & 1, row & 15
    stencil[256:384, :] = jnp.where(rp == cz, bias(rj - 2 - cy), 0.0).astype(BF16)
    stencil[384:512, :] = jnp.where(rp == cz, bias(rj + 16 - cy), 0.0).astype(BF16)
    zat = jnp.where(iz == 0, 16, -2)
    stencil[512:640, :] = jnp.where(rp == cy, bias(rj + zat - cz), 0.0).astype(BF16)

    for copy in small:
        copy.wait()

    for i in range(CUBE):
        line = potv[0:1, PLANE * i : PLANE * (i + 1)]
        pterm[16 * i : 16 * i + 16, :] = jnp.broadcast_to(0.25 * (line - 2.25), (16, PLANE))

    for pair in range(2):
        flats = []
        for a in (2 * pair, 2 * pair + 1):
            where = ptv[a : a + 1, :]
            upper, lower = where >> 7, where & 127
            hot = jnp.where(iota((128, 256), 0) == lower, one, nil).astype(BF16)
            values = projv[a]
            lead = values.astype(BF16).astype(F32)
            parts = jnp.concatenate([lead, values - lead], axis=0)
            spread = jnp.concatenate(
                [jnp.where(upper == h, parts, nil).astype(BF16) for h in range(32)], axis=0
            )
            dense = dot(spread, hot, 1, 1)
            flats.append(
                [dense[16 * h : 16 * h + 8, :] + dense[16 * h + 8 : 16 * h + 16, :] for h in range(32)]
            )
            couple[8 * a : 8 * a + 8, 8 * a : 8 * a + 8] = 0.25 * coupv[a]
        for h in range(32):
            fh, fl = split(jnp.concatenate([flats[0][h], flats[1][h]], axis=0))
            here = slice(128 * h, 128 * h + 128)
            bcat[16 * pair : 16 * pair + 16, here] = fh
            bcat[32 + 16 * pair : 48 + 16 * pair, here] = fl
            bcat[64 + 16 * pair : 80 + 16 * pair, here] = fh

    vx1[32:288, :] = inside(vx0) + outside(0, vx0)
    send_faces(1, vx1, (3, 4))
    pack_y(1, vx1)
    send_faces(1, vx1, (0, 1))
    pack_z(1, vx1)
    send_faces(1, vx1, (2,))
    fs[...] = 2.0 * (inside(vx1) + outside(1, vx1)) - vx0[32:288, :]

    def to_piece(peer):
        return pltpu.make_async_remote_copy(
            src_ref=fs.at[pl.ds(pl.multiple_of(peer * 16, 16), 16), :],
            dst_ref=work.at[pl.ds(pl.multiple_of(band * 16, 16), 16), pl.ds(PLANE, PLANE)],
            send_sem=a_send.at[peer], recv_sem=a_recv.at[band],
            device_id=(dom, peer), device_id_type=MESH,
        )

    def from_piece(peer):
        return pltpu.make_async_remote_copy(
            src_ref=fs.at[pl.ds(0, 16), :],
            dst_ref=work.at[pl.ds(pl.multiple_of(peer * 16, 16), 16), pl.ds(PLANE, PLANE)],
            send_sem=a_send.at[peer], recv_sem=a_recv.at[peer],
            device_id=(dom, peer), device_id_type=MESH,
        )

    def each(count, me, action):
        for k in range(count - 1):
            step = count // 2 + (1 - 2 * (k % 2)) * ((k + 1) // 2)
            action(lax.rem(me + step, count))

    def peers(count, me, action):
        @pl.loop(0, count - 1)
        def _(k):
            step = count // 2 + (1 - 2 * lax.rem(k, 2)) * ((k + 1) // 2)
            action(lax.rem(me + step, count))

    each(NBAND, band, lambda peer: to_piece(peer).start())
    mine = pl.ds(pl.multiple_of(band * 16, 16), 16)
    work[mine, PLANE : 2 * PLANE] = fs[mine, :]
    each(NBAND, band, lambda peer: from_piece(peer).wait_recv())

    piece = work[:, PLANE : 2 * PLANE]
    ph, plo = split(piece)
    def product(i, n):
        h, l = ph[i : i + 128], plo[i : i + 128]
        return (1.0 / POINTS) * (
            dot(h, ph[0:n], 1, 1) + (dot(h, plo[0:n], 1, 1) + dot(l, ph[0:n], 1, 1))
        )

    upper, lower = product(0, 128), product(128, 256)
    row, col = iota((128, 128), 0), iota((128, 128), 1)
    low = lower[:, 128:256]
    packed = jnp.where(row >= col, upper, low)
    diag = jnp.sum(jnp.where(row == col, low, 0.0), axis=0, keepdims=True)
    for c in range(NSET):
        part[c, 0:16, :] = packed[16 * c : 16 * c + 16, :]
        part[c, 16:32, :] = lower[16 * c : 16 * c + 16, 0:128]
        part[c, 32:33, :] = diag

    def chunk(src, dst, send, recv, where):
        return pltpu.make_async_remote_copy(
            src_ref=src, dst_ref=dst, send_sem=send, recv_sem=recv, device_id=where, device_id_type=MESH
        )

    def share(count, me, at, buf, send, recv):
        each(count, me, lambda peer: chunk(
            buf.at[me], buf.at[me], send.at[peer], recv.at[me], at(peer)).start())

    def collect(count, me, at, buf, send, recv):
        each(count, me, lambda peer: chunk(
            buf.at[me], buf.at[peer], send.at[peer], recv.at[peer], at(peer)).wait_recv())

    def drain(count, me, at, buf, send, recv):
        peers(count, me, lambda peer: chunk(
            buf.at[me], buf.at[peer], send.at[peer], recv.at[peer], at(peer)).wait_send())

    def total(buf, count):
        value = buf[0]
        for i in range(1, count):
            value = value + buf[i]
        return value

    each(NSET, mine_set, lambda peer: chunk(
        part.at[peer], rs_buf.at[mine_set], r_send.at[peer], r_recv.at[mine_set], at_set(peer)).start())
    rs_buf[mine_set] = part[mine_set]
    each(NSET, mine_set, lambda peer: chunk(
        part.at[peer], rs_buf.at[peer], r_send.at[peer], r_recv.at[peer], at_set(peer)).wait_recv())
    value = total(rs_buf, NSET)
    a_y = (NY, py, at_y, ay_buf, s_send.at[0], s_recv.at[0])
    b_z = (NZ, pz, at_z, bz_buf, s_send.at[1], s_recv.at[1])
    a_z = (NZ, pz, at_z, az_buf, s_send.at[2], s_recv.at[2])
    b_y = (NY, py, at_y, by_buf, s_send.at[3], s_recv.at[3])
    a_set = (NSET, mine_set, at_set, g_buf, s_send.at[4], s_recv.at[4])
    ay_buf[py] = value[0:16]
    share(*a_y)
    bz_buf[pz] = value[16:33]
    share(*b_z)
    collect(*a_y)
    az_buf[pz] = total(ay_buf, NY)
    share(*a_z)
    collect(*b_z)
    by_buf[py] = total(bz_buf, NZ)
    share(*b_y)
    collect(*a_z)
    g_buf[mine_set, 0:16, :] = total(az_buf, NZ)
    collect(*b_y)
    g_buf[mine_set, 16:33, :] = total(by_buf, NY)
    share(*a_set)
    collect(*a_set)

    packed = jnp.concatenate([g_buf[c, 0:16, :] for c in range(NSET)], axis=0)
    cross = jnp.concatenate([g_buf[c, 16:32, :] for c in range(NSET)], axis=0)
    diag = jnp.broadcast_to(g_buf[0, 32:33, :], (128, 128))
    turned = packed.T
    work[0:128, 0:128] = jnp.where(row >= col, packed, turned)
    work[128:256, 128:256] = jnp.where(row < col, packed, jnp.where(row == col, diag, turned))
    work[128:256, 0:128] = cross
    work[0:128, 128:256] = cross.T

    def to_out(peer, half):
        return pltpu.make_async_remote_copy(
            src_ref=fs.at[pl.ds(pl.multiple_of(peer * 16 + 8 * half, 8), 8), :],
            dst_ref=out.at[pl.ds(8 * half, 8), pl.ds(pl.multiple_of(band * PLANE, PLANE), PLANE)],
            send_sem=o_send.at[half, peer], recv_sem=o_recv.at[half, band],
            device_id=(dom, peer), device_id_type=MESH,
        )

    def from_out(peer, half):
        return pltpu.make_async_remote_copy(
            src_ref=fs.at[pl.ds(0, 8), :],
            dst_ref=out.at[pl.ds(8 * half, 8), pl.ds(pl.multiple_of(peer * PLANE, PLANE), PLANE)],
            send_sem=o_send.at[half, peer], recv_sem=o_recv.at[half, peer],
            device_id=(dom, peer), device_id_type=MESH,
        )

    peers(NBAND, band, lambda peer: to_piece(peer).wait_send())

    srow = iota((8, 128), 0)

    def spread_row(value, k):
        return jnp.broadcast_to(value[k : k + 1, :], (8, 128))

    for j in range(256 // BLOCK):
        first = j * BLOCK
        lo = first // 128 * 128
        count = BLOCK // 8
        tiles = [
            [work[first + 8 * t : first + 8 * t + 8, c : c + 128] for c in range(lo, 512, 128)]
            for t in range(count)
        ]

        def columns(s, start):
            at = first - lo + 8 * s
            return {
                t: [jnp.broadcast_to(tiles[t][0][:, at + k : at + k + 1], (8, 128)) for k in range(8)]
                for t in range(start, count)
            }

        cols = columns(0, 0)
        for s in range(count):
            coming = columns(s + 1, s) if s + 1 < count else None
            factors = []
            pivot = spread_row(cols[s][0], 0)
            pivots = pivot
            for k in range(8):
                inverse = 1.0 / pivot
                heads = {m: spread_row(cols[s][m], k) for m in range(k + 1, 8)}
                lead = [spread_row(v, k) for v in tiles[s]]
                if k < 7:
                    pivot = spread_row(cols[s][k + 1], k + 1) - (
                        spread_row(cols[s][k], k + 1) * inverse
                    ) * heads[k + 1]
                    pivots = jnp.where(srow > k, pivot, pivots)
                factor = {
                    t: (jnp.where(srow > k, cols[s][k], 0.0) if t == s else cols[t][k]) * inverse
                    for t in range(s, count)
                    if t != s or k < 7
                }
                factors.append(factor)
                for t in factor:
                    for m in range(k + 1, 8):
                        cols[t][m] = cols[t][m] - factor[t] * heads[m]
                    tiles[t] = [v - factor[t] * r for v, r in zip(tiles[t], lead)]
            if coming is not None:
                for k in range(8):
                    heads = [spread_row(coming[s][m], k) for m in range(8)]
                    for t in factors[k]:
                        for m in range(8):
                            coming[t][m] = coming[t][m] - factors[k][t] * heads[m]
                cols = coming
            scale = lax.rsqrt(pivots)
            tiles[s] = [v * scale for v in tiles[s]]
            fs[first + 8 * s : first + 8 * s + 8, 0:128] = tiles[s][-2]
            fs[first + 8 * s : first + 8 * s + 8, 128:256] = tiles[s][-1]
            peer = j * (BLOCK // 16) + s // 2
            pl.when(peer != band)(to_out(peer, s % 2).start)
        lanes = [jnp.concatenate([tiles[t][c] for t in range(count)], axis=0) for c in range((512 - lo) // 128)]

        after = first + BLOCK
        if after < 256:
            base = after // 128 * 128
            rest = jnp.concatenate(lanes[(base - lo) // 128 :], axis=1)
            high, low = split(rest)
            lead = high[:, 0 : 256 - base].astype(F32)
            left = jnp.concatenate([lead, lead, rest[:, 0 : 256 - base] - lead], axis=0).T
            left = left[after - base :, :].astype(BF16)
            work[after:256, base:512] = work[after:256, base:512] - dot(
                left, jnp.concatenate([high, low, high], axis=0)
            )

    own = pltpu.make_async_copy(
        fs.at[mine, :], out.at[:, pl.ds(pl.multiple_of(band * PLANE, PLANE), PLANE)], o_own
    )
    own.start()
    for turn, ref in ((0, vx0), (1, vx1)):
        for face in halo(turn, ref):
            under(face[0], face[2].wait_send)
    peers(NSET, mine_set, lambda peer: chunk(
        part.at[peer], rs_buf.at[peer], r_send.at[peer], r_recv.at[peer], at_set(peer)).wait_send())
    for stage in (a_y, b_z, a_z, b_y, a_set):
        drain(*stage)
    for half in range(2):
        peers(NBAND, band, lambda peer: from_out(peer, half).wait_recv())
    for half in range(2):
        peers(NBAND, band, lambda peer: to_out(peer, half).wait_send())
    own.wait()


def local(waves, potential, atom_points, projectors, coupling):
    dma = pltpu.SemaphoreType.DMA
    vmem = pltpu.VMEM
    return pl.pallas_call(
        kernel,
        out_shape=jax.ShapeDtypeStruct((BAND_LOC, CUBE**3), F32),
        in_specs=[pl.BlockSpec(memory_space=pltpu.MemorySpace.HBM)] * 5,
        out_specs=pl.BlockSpec(memory_space=pl.ANY),
        scratch_shapes=[
            vmem((320, 256), F32), vmem((320, 256), F32), vmem((256, 256), F32),
            vmem((2, 3, 64, 128), F32), vmem((2, 3, 64, 128), F32),
            vmem((256, 128), BF16), vmem((640, 256), BF16),
            vmem((96, 4096), BF16), vmem((32, 32), F32),
            vmem((256, 256), F32), vmem((256, 512), F32),
            vmem((4, 256), jnp.int32), vmem((4, 8, 256), F32), vmem((4, 8, 8), F32), vmem((1, 4096), F32),
            vmem((NSET, ROWS, 128), F32), vmem((NSET, ROWS, 128), F32),
            vmem((NY, 16, 128), F32), vmem((NZ, 16, 128), F32),
            vmem((NZ, 17, 128), F32), vmem((NY, 17, 128), F32), vmem((NSET, ROWS, 128), F32),
            dma((20,)), dma((2, 5)), dma((2, 5)), dma((16,)), dma((16,)), dma((8,)), dma((8,)),
            dma((5, 8)), dma((5, 8)), dma((2, 16)), dma((2, 16)), dma,
        ],
        compiler_params=pltpu.CompilerParams(collective_id=0, has_side_effects=True, vmem_limit_bytes=12 << 20),
    )(
        *(
            pltpu.with_memory_space_constraint(value, pltpu.MemorySpace.HBM)
            for value in (waves, potential.reshape(1, CUBE**3), atom_points, projectors, coupling)
        )
    )


def solution(mesh):
    placed = (
        P("band", "dom"),
        P("dom"),
        P("dom", None),
        P("dom", None, None),
        P("dom", None, None),
    )
    return jax.shard_map(
        local, mesh=mesh, in_specs=placed, out_specs=P("band", "dom"), check_vma=False
    )
```

```python
import jax
import jax.numpy as jnp
from jax import lax
from jax.experimental import pallas as pl
from jax.experimental.pallas import tpu as pltpu
from jax.sharding import PartitionSpec as P

F32, BF16 = jnp.float32, jnp.bfloat16
MESH = pl.DeviceIdType.MESH
CUBE = 16
BAND_LOC = 16
PLANE = CUBE * CUBE
POINTS = 131072
NBAND, NZ, NY, NX, NSET = 16, 8, 8, 4, 8
ROWS = 33
BLOCK = 32


def iota(shape, dim):
    return lax.broadcasted_iota(jnp.int32, shape, dim)


def split(x):
    big = x.astype(BF16)
    return big, (x - big.astype(F32)).astype(BF16)


def dot(a, b, ca=1, cb=0):
    return lax.dot_general(a, b, (((ca,), (cb,)), ((), ())), preferred_element_type=F32)


def bias(delta):
    step = jnp.abs(delta)
    return jnp.where(step == 1, -16.0, jnp.where(step == 2, 1.0, 0.0))


def kernel(
    waves, pot, pts, proj, coup, out,
    vx0, vx1, pterm, facesend, facerecv, pick, stencil, bcat, couple, fs, work,
    ptv, projv, coupv, potv, part, rs_buf, ay_buf, az_buf, bz_buf, by_buf, g_buf,
    in_sem, h_send, h_recv, a_send, a_recv, r_send, r_recv, s_send, s_recv, o_send, o_recv, o_own,
):
    dom, band = lax.axis_index("dom"), lax.axis_index("band")
    pz, px = dom // NX, lax.rem(dom, NX)
    py, core = band // 2, lax.rem(band, 2)
    mine_set = px * 2 + core
    iz = lax.rem(dom, 2)
    iy = lax.rem(dom // 2, 4)
    ix = dom // 8
    middle = jnp.logical_or(iy == 1, iy == 2)

    copies = [
        pltpu.make_async_copy(
            waves.at[:, pl.ds(PLANE * i, PLANE)], vx0.at[pl.ds(32 + 16 * i, 16), :], in_sem.at[i]
        )
        for i in range(CUBE)
    ]
    small = [
        pltpu.make_async_copy(src, dst, in_sem.at[16 + i])
        for i, (src, dst) in enumerate(((pts, ptv), (proj, projv), (coup, coupv), (pot, potv)))
    ]
    for copy in copies + small:
        copy.start()

    facerecv[...] = jnp.zeros_like(facerecv)
    couple[...] = jnp.zeros_like(couple)
    for ref in (vx0, vx1):
        ref[0:32, :] = jnp.zeros((32, PLANE), F32)
        ref[288:320, :] = jnp.zeros((32, PLANE), F32)

    def at_band(peer):
        return (dom, peer)

    def at_y(peer):
        return (dom, peer * 2 + core)

    def at_z(peer):
        return (peer * NX + px, band)

    def at_set(peer):
        return (pz * NX + peer // 2, py * 2 + lax.rem(peer, 2))

    barrier = pltpu.get_barrier_semaphore()

    def greet(where):
        pl.semaphore_signal(barrier, inc=1, device_id=where, device_id_type=MESH)

    @pl.loop(1, NBAND)
    def _(k):
        greet((dom, lax.rem(band + k, NBAND)))

    @pl.loop(1, NZ)
    def _(k):
        greet((lax.rem(pz + k, NZ) * NX + px, band))

    @pl.loop(1, NSET)
    def _(k):
        greet(at_set(lax.rem(mine_set + k, NSET)))

    @pl.when(iy == 1)
    def _():
        greet((dom + 2, band))

    @pl.when(iy == 2)
    def _():
        greet((dom - 2, band))

    group = iota((64, 128), 1) >> 5

    def halo(turn, ref):
        def face(slot, src, dst, where):
            return pltpu.make_async_remote_copy(
                src_ref=src, dst_ref=dst, send_sem=h_send.at[turn, slot],
                recv_sem=h_recv.at[turn, slot], device_id=(where, band), device_id_type=MESH,
            )
        return (
            (iy > 0, iy < 3, face(0, facesend.at[turn, 0], facerecv.at[turn, 1], dom - 2)),
            (iy < 3, iy > 0, face(1, facesend.at[turn, 1], facerecv.at[turn, 0], dom + 2)),
            (None, None, face(2, facesend.at[turn, 2], facerecv.at[turn, 2], dom + 1 - 2 * iz)),
            (ix > 0, ix < 3, face(3, ref.at[pl.ds(32, 32), :], ref.at[pl.ds(288, 32), :], dom - 8)),
            (ix < 3, ix > 0, face(4, ref.at[pl.ds(256, 32), :], ref.at[pl.ds(0, 32), :], dom + 8)),
        )

    def under(condition, action):
        if condition is None:
            action()
        else:
            pl.when(condition)(action)

    def pack_y(turn, ref):
        for slot, at in ((0, 0), (1, 128)):
            packed = None
            for g in range(4):
                shift = (32 * g + 32 * slot) % 128
                part = ref[32 + 64 * g : 96 + 64 * g, at : at + 128]
                part = pltpu.roll(part, shift, 1) if shift else part
                packed = part if g == 0 else jnp.where(group == g, part, packed)
            facesend[turn, slot] = packed

    def pack_z(turn, ref):
        vh, vl = split(ref[32:288, :])
        ends = dot(vh, pick[...]) + dot(vl, pick[...])
        packed = ends[0:64, :]
        for g in range(1, 4):
            packed = jnp.where(group == g, ends[64 * g : 64 * g + 64, :], packed)
        facesend[turn, 2] = packed

    def send_faces(turn, ref, slots):
        faces = halo(turn, ref)
        for slot in slots:
            under(faces[slot][0], faces[slot][2].start)

    def inside(ref):
        here = ref[32:288, :]
        vh, vl = split(here)
        both = jnp.concatenate(
            [jnp.concatenate([v[16 * i : 16 * i + 16, :] for i in range(CUBE)], axis=1) for v in (vh, vl)],
            axis=0,
        )
        quad = dot(both, bcat[0:64, :], 1, 1)
        coef = quad[0:16, 0:32] + (quad[0:16, 32:64] + quad[16:32, 0:32])
        ch, cl = split(coef)
        kh, kl = split(couple[...])
        ch, cl = split(dot(ch, kh, 1, 1) + (dot(ch, kl, 1, 1) + dot(cl, kh, 1, 1)))
        added = dot(jnp.concatenate([ch, ch, cl], axis=1), bcat[...])
        added = jnp.concatenate([added[:, PLANE * i : PLANE * (i + 1)] for i in range(CUBE)], axis=0)
        inner = dot(vh, stencil[0:256, :]) + dot(vl, stencil[0:256, :])
        return pterm[...] * here + added + (1.0 / 96.0) * inner

    def from_faces(turn, slots):
        wide = jnp.concatenate(
            [
                jnp.concatenate(
                    [jnp.where(group == g, facerecv[turn, slot], 0.0) for g in range(4)], axis=0
                )
                for slot in slots
            ],
            axis=1,
        )
        wh, wl = split(wide)
        table = stencil[256 + 128 * slots[0] : 384 + 128 * slots[-1], :]
        return jnp.concatenate(
            [dot(wh[r : r + 128], table) + dot(wl[r : r + 128], table) for r in (0, 128)], axis=0
        )

    def outside(turn, ref):
        faces = halo(turn, ref)
        for slot in (2, 3, 4):
            under(faces[slot][1], faces[slot][2].wait_recv)
        far = ref[0:256, :] + ref[64:320, :]
        near = ref[16:272, :] + ref[48:304, :]
        value = from_faces(turn, (2,)) + (far - 16.0 * near)
        for slot in (0, 1):
            under(faces[slot][1], faces[slot][2].wait_recv)
        return (1.0 / 96.0) * (value + from_faces(turn, (0, 1)))

    row, col = iota((PLANE, 128), 0), iota((PLANE, 128), 1)
    ry, rz = row >> 4, row & 15
    cj, cp = (col >> 4) & 1, col & 15
    one, nil = jnp.float32(1), jnp.float32(0)
    zlo = jnp.where(iz == 0, 14, 0)
    pick[...] = jnp.where(row == cp * 16 + cj + zlo, one, nil).astype(BF16)

    for copy in copies:
        copy.wait()
    pack_y(0, vx0)
    pack_z(0, vx0)
    pl.semaphore_wait(barrier, 29 + middle.astype(jnp.int32))
    send_faces(0, vx0, range(5))

    row, col = iota((PLANE, PLANE), 0), iota((PLANE, PLANE), 1)
    ry, rz, cy, cz = row >> 4, row & 15, col >> 4, col & 15
    stencil[0:256, :] = (
        jnp.where(rz == cz, bias(ry - cy), 0.0) + jnp.where(ry == cy, bias(rz - cz), 0.0)
    ).astype(BF16)
    row, col = iota((128, PLANE), 0), iota((128, PLANE), 1)
    cy, cz = col >> 4, col & 15
    rj, rp = (row >> 4) & 1, row & 15
    stencil[256:384, :] = jnp.where(rp == cz, bias(rj - 2 - cy), 0.0).astype(BF16)
    stencil[384:512, :] = jnp.where(rp == cz, bias(rj + 16 - cy), 0.0).astype(BF16)
    zat = jnp.where(iz == 0, 16, -2)
    stencil[512:640, :] = jnp.where(rp == cy, bias(rj + zat - cz), 0.0).astype(BF16)

    for copy in small:
        copy.wait()

    for i in range(CUBE):
        line = potv[0:1, PLANE * i : PLANE * (i + 1)]
        pterm[16 * i : 16 * i + 16, :] = jnp.broadcast_to(0.25 * (line - 2.25), (16, PLANE))

    for pair in range(2):
        flats = []
        for a in (2 * pair, 2 * pair + 1):
            where = ptv[a : a + 1, :]
            upper, lower = where >> 7, where & 127
            hot = jnp.where(iota((128, 256), 0) == lower, one, nil).astype(BF16)
            values = projv[a]
            lead = values.astype(BF16).astype(F32)
            parts = jnp.concatenate([lead, values - lead], axis=0)
            spread = jnp.concatenate(
                [jnp.where(upper == h, parts, nil).astype(BF16) for h in range(32)], axis=0
            )
            dense = dot(spread, hot, 1, 1)
            flats.append(
                [dense[16 * h : 16 * h + 8, :] + dense[16 * h + 8 : 16 * h + 16, :] for h in range(32)]
            )
            couple[8 * a : 8 * a + 8, 8 * a : 8 * a + 8] = 0.25 * coupv[a]
        for h in range(32):
            fh, fl = split(jnp.concatenate([flats[0][h], flats[1][h]], axis=0))
            here = slice(128 * h, 128 * h + 128)
            bcat[16 * pair : 16 * pair + 16, here] = fh
            bcat[32 + 16 * pair : 48 + 16 * pair, here] = fl
            bcat[64 + 16 * pair : 80 + 16 * pair, here] = fh

    vx1[32:288, :] = inside(vx0) + outside(0, vx0)
    send_faces(1, vx1, (3, 4))
    pack_y(1, vx1)
    send_faces(1, vx1, (0, 1))
    pack_z(1, vx1)
    send_faces(1, vx1, (2,))
    fs[...] = 2.0 * (inside(vx1) + outside(1, vx1)) - vx0[32:288, :]

    def to_piece(peer):
        return pltpu.make_async_remote_copy(
            src_ref=fs.at[pl.ds(pl.multiple_of(peer * 16, 16), 16), :],
            dst_ref=work.at[pl.ds(pl.multiple_of(band * 16, 16), 16), pl.ds(PLANE, PLANE)],
            send_sem=a_send.at[peer], recv_sem=a_recv.at[band],
            device_id=(dom, peer), device_id_type=MESH,
        )

    def from_piece(peer):
        return pltpu.make_async_remote_copy(
            src_ref=fs.at[pl.ds(0, 16), :],
            dst_ref=work.at[pl.ds(pl.multiple_of(peer * 16, 16), 16), pl.ds(PLANE, PLANE)],
            send_sem=a_send.at[peer], recv_sem=a_recv.at[peer],
            device_id=(dom, peer), device_id_type=MESH,
        )

    def each(count, me, action):
        for k in range(count - 1):
            step = count // 2 + (1 - 2 * (k % 2)) * ((k + 1) // 2)
            action(lax.rem(me + step, count))

    def peers(count, me, action):
        @pl.loop(0, count - 1)
        def _(k):
            step = count // 2 + (1 - 2 * lax.rem(k, 2)) * ((k + 1) // 2)
            action(lax.rem(me + step, count))

    each(NBAND, band, lambda peer: to_piece(peer).start())
    mine = pl.ds(pl.multiple_of(band * 16, 16), 16)
    work[mine, PLANE : 2 * PLANE] = fs[mine, :]
    each(NBAND, band, lambda peer: from_piece(peer).wait_recv())

    piece = work[:, PLANE : 2 * PLANE]
    ph, plo = split(piece)
    def product(i, n):
        h, l = ph[i : i + 128], plo[i : i + 128]
        return (1.0 / POINTS) * (
            dot(h, ph[0:n], 1, 1) + (dot(h, plo[0:n], 1, 1) + dot(l, ph[0:n], 1, 1))
        )

    upper, lower = product(0, 128), product(128, 256)
    row, col = iota((128, 128), 0), iota((128, 128), 1)
    low = lower[:, 128:256]
    packed = jnp.where(row >= col, upper, low)
    diag = jnp.sum(jnp.where(row == col, low, 0.0), axis=0, keepdims=True)
    for c in range(NSET):
        part[c, 0:16, :] = packed[16 * c : 16 * c + 16, :]
        part[c, 16:32, :] = lower[16 * c : 16 * c + 16, 0:128]
        part[c, 32:33, :] = diag

    def chunk(src, dst, send, recv, where):
        return pltpu.make_async_remote_copy(
            src_ref=src, dst_ref=dst, send_sem=send, recv_sem=recv, device_id=where, device_id_type=MESH
        )

    def share(count, me, at, buf, send, recv):
        each(count, me, lambda peer: chunk(
            buf.at[me], buf.at[me], send.at[peer], recv.at[me], at(peer)).start())

    def collect(count, me, at, buf, send, recv):
        each(count, me, lambda peer: chunk(
            buf.at[me], buf.at[peer], send.at[peer], recv.at[peer], at(peer)).wait_recv())

    def drain(count, me, at, buf, send, recv):
        peers(count, me, lambda peer: chunk(
            buf.at[me], buf.at[peer], send.at[peer], recv.at[peer], at(peer)).wait_send())

    def total(buf, count):
        value = buf[0]
        for i in range(1, count):
            value = value + buf[i]
        return value

    each(NSET, mine_set, lambda peer: chunk(
        part.at[peer], rs_buf.at[mine_set], r_send.at[peer], r_recv.at[mine_set], at_set(peer)).start())
    rs_buf[mine_set] = part[mine_set]
    each(NSET, mine_set, lambda peer: chunk(
        part.at[peer], rs_buf.at[peer], r_send.at[peer], r_recv.at[peer], at_set(peer)).wait_recv())
    value = total(rs_buf, NSET)
    a_y = (NY, py, at_y, ay_buf, s_send.at[0], s_recv.at[0])
    b_z = (NZ, pz, at_z, bz_buf, s_send.at[1], s_recv.at[1])
    a_z = (NZ, pz, at_z, az_buf, s_send.at[2], s_recv.at[2])
    b_y = (NY, py, at_y, by_buf, s_send.at[3], s_recv.at[3])
    a_set = (NSET, mine_set, at_set, g_buf, s_send.at[4], s_recv.at[4])
    ay_buf[py] = value[0:16]
    share(*a_y)
    bz_buf[pz] = value[16:33]
    share(*b_z)
    collect(*a_y)
    az_buf[pz] = total(ay_buf, NY)
    share(*a_z)
    collect(*b_z)
    by_buf[py] = total(bz_buf, NZ)
    share(*b_y)
    collect(*a_z)
    g_buf[mine_set, 0:16, :] = total(az_buf, NZ)
    collect(*b_y)
    g_buf[mine_set, 16:33, :] = total(by_buf, NY)
    share(*a_set)
    collect(*a_set)

    packed = jnp.concatenate([g_buf[c, 0:16, :] for c in range(NSET)], axis=0)
    cross = jnp.concatenate([g_buf[c, 16:32, :] for c in range(NSET)], axis=0)
    diag = jnp.broadcast_to(g_buf[0, 32:33, :], (128, 128))
    turned = packed.T
    work[0:128, 0:128] = jnp.where(row >= col, packed, turned)
    work[128:256, 128:256] = jnp.where(row < col, packed, jnp.where(row == col, diag, turned))
    work[128:256, 0:128] = cross
    work[0:128, 128:256] = cross.T

    def to_out(peer, half):
        return pltpu.make_async_remote_copy(
            src_ref=fs.at[pl.ds(pl.multiple_of(peer * 16 + 8 * half, 8), 8), :],
            dst_ref=out.at[pl.ds(8 * half, 8), pl.ds(pl.multiple_of(band * PLANE, PLANE), PLANE)],
            send_sem=o_send.at[half, peer], recv_sem=o_recv.at[half, band],
            device_id=(dom, peer), device_id_type=MESH,
        )

    def from_out(peer, half):
        return pltpu.make_async_remote_copy(
            src_ref=fs.at[pl.ds(0, 8), :],
            dst_ref=out.at[pl.ds(8 * half, 8), pl.ds(pl.multiple_of(peer * PLANE, PLANE), PLANE)],
            send_sem=o_send.at[half, peer], recv_sem=o_recv.at[half, peer],
            device_id=(dom, peer), device_id_type=MESH,
        )

    peers(NBAND, band, lambda peer: to_piece(peer).wait_send())

    srow = iota((8, 128), 0)

    def spread_row(value, k):
        return jnp.broadcast_to(value[k : k + 1, :], (8, 128))

    for j in range(256 // BLOCK):
        first = j * BLOCK
        lo = first // 128 * 128
        count = BLOCK // 8
        tiles = [
            [work[first + 8 * t : first + 8 * t + 8, c : c + 128] for c in range(lo, 512, 128)]
            for t in range(count)
        ]

        def columns(s, start):
            at = first - lo + 8 * s
            return {
                t: [jnp.broadcast_to(tiles[t][0][:, at + k : at + k + 1], (8, 128)) for k in range(8)]
                for t in range(start, count)
            }

        cols = columns(0, 0)
        for s in range(count):
            coming = columns(s + 1, s) if s + 1 < count else None
            factors = []
            pivot = spread_row(cols[s][0], 0)
            pivots = pivot
            for k in range(8):
                inverse = 1.0 / pivot
                heads = {m: spread_row(cols[s][m], k) for m in range(k + 1, 8)}
                lead = [spread_row(v, k) for v in tiles[s]]
                if k < 7:
                    pivot = spread_row(cols[s][k + 1], k + 1) - (
                        spread_row(cols[s][k], k + 1) * inverse
                    ) * heads[k + 1]
                    pivots = jnp.where(srow > k, pivot, pivots)
                factor = {
                    t: (jnp.where(srow > k, cols[s][k], 0.0) if t == s else cols[t][k]) * inverse
                    for t in range(s, count)
                    if t != s or k < 7
                }
                factors.append(factor)
                for t in factor:
                    for m in range(k + 1, 8):
                        cols[t][m] = cols[t][m] - factor[t] * heads[m]
                    tiles[t] = [v - factor[t] * r for v, r in zip(tiles[t], lead)]
            if coming is not None:
                for k in range(8):
                    heads = [spread_row(coming[s][m], k) for m in range(8)]
                    for t in factors[k]:
                        for m in range(8):
                            coming[t][m] = coming[t][m] - factors[k][t] * heads[m]
                cols = coming
            scale = lax.rsqrt(pivots)
            tiles[s] = [v * scale for v in tiles[s]]
            fs[first + 8 * s : first + 8 * s + 8, 0:128] = tiles[s][-2]
            fs[first + 8 * s : first + 8 * s + 8, 128:256] = tiles[s][-1]
            peer = j * (BLOCK // 16) + s // 2
            pl.when(peer != band)(to_out(peer, s % 2).start)
        lanes = [jnp.concatenate([tiles[t][c] for t in range(count)], axis=0) for c in range((512 - lo) // 128)]

        after = first + BLOCK
        if after < 256:
            base = after // 128 * 128
            rest = jnp.concatenate(lanes[(base - lo) // 128 :], axis=1)
            high, low = split(rest)
            left = jnp.concatenate([high, high, low], axis=0)[:, 0 : 256 - base]
            update = dot(left, jnp.concatenate([high, low, high], axis=0), 0, 0)
            work[after:256, base:512] = work[after:256, base:512] - update[after - base :]

    own = pltpu.make_async_copy(
        fs.at[mine, :], out.at[:, pl.ds(pl.multiple_of(band * PLANE, PLANE), PLANE)], o_own
    )
    own.start()
    for turn, ref in ((0, vx0), (1, vx1)):
        for face in halo(turn, ref):
            under(face[0], face[2].wait_send)
    peers(NSET, mine_set, lambda peer: chunk(
        part.at[peer], rs_buf.at[peer], r_send.at[peer], r_recv.at[peer], at_set(peer)).wait_send())
    for stage in (a_y, b_z, a_z, b_y, a_set):
        drain(*stage)
    own.wait()
    for half in range(2):
        peers(NBAND, band, lambda peer: to_out(peer, half).wait_send())
    for half in range(2):
        each(NBAND, band, lambda peer: from_out(peer, half).wait_recv())


def local(waves, potential, atom_points, projectors, coupling):
    dma = pltpu.SemaphoreType.DMA
    vmem = pltpu.VMEM
    return pl.pallas_call(
        kernel,
        out_shape=jax.ShapeDtypeStruct((BAND_LOC, CUBE**3), F32),
        in_specs=[pl.BlockSpec(memory_space=pltpu.MemorySpace.HBM)] * 5,
        out_specs=pl.BlockSpec(memory_space=pl.ANY),
        scratch_shapes=[
            vmem((320, 256), F32), vmem((320, 256), F32), vmem((256, 256), F32),
            vmem((2, 3, 64, 128), F32), vmem((2, 3, 64, 128), F32),
            vmem((256, 128), BF16), vmem((640, 256), BF16),
            vmem((96, 4096), BF16), vmem((32, 32), F32),
            vmem((256, 256), F32), vmem((256, 512), F32),
            vmem((4, 256), jnp.int32), vmem((4, 8, 256), F32), vmem((4, 8, 8), F32), vmem((1, 4096), F32),
            vmem((NSET, ROWS, 128), F32), vmem((NSET, ROWS, 128), F32),
            vmem((NY, 16, 128), F32), vmem((NZ, 16, 128), F32),
            vmem((NZ, 17, 128), F32), vmem((NY, 17, 128), F32), vmem((NSET, ROWS, 128), F32),
            dma((20,)), dma((2, 5)), dma((2, 5)), dma((16,)), dma((16,)), dma((8,)), dma((8,)),
            dma((5, 8)), dma((5, 8)), dma((2, 16)), dma((2, 16)), dma,
        ],
        compiler_params=pltpu.CompilerParams(collective_id=0, has_side_effects=True, vmem_limit_bytes=12 << 20),
    )(
        *(
            pltpu.with_memory_space_constraint(value, pltpu.MemorySpace.HBM)
            for value in (waves, potential.reshape(1, CUBE**3), atom_points, projectors, coupling)
        )
    )


def solution(mesh):
    placed = (
        P("band", "dom"),
        P("dom"),
        P("dom", None),
        P("dom", None, None),
        P("dom", None, None),
    )
    return jax.shard_map(
        local, mesh=mesh, in_specs=placed, out_specs=P("band", "dom"), check_vma=False
    )
```
